128 devices in a mesh: section: 8 (over x, core), expert: 16 (over y, z).
Axes of the slice: x: 4, y: 4, z: 4, core: 2. Of those that a mesh axis runs over, the one named last changes fastest.
Arguments:
- act_in: bfloat16 [8, 2048, 6144], P('section', 'expert'), may hold values from -6 to 6
- saved_in: bfloat16 [8, 2048, 6144], P('section', 'expert'), may hold values from -6 to 6
- grad_in: bfloat16 [8, 2048, 6144], P('section', 'expert'), may hold values from -6 to 6
- fwd_routes: int32 [8, 2048, 2], P('section', 'expert'), may hold values from 0 to 7, as said below
- bwd_routes: int32 [8, 2048, 2], P('section', 'expert'), may hold values from 0 to 7, as said below
- w_gate: bfloat16 [8, 6144, 8192], P('section', None, 'expert'), may hold values from -0.078125 to 0.078125
- w_up: bfloat16 [8, 6144, 8192], P('section', None, 'expert'), may hold values from -0.078125 to 0.078125
- w_down: bfloat16 [8, 8192, 6144], P('section', 'expert'), may hold values from -0.0625 to 0.0625
- router: float32 [8, 6144, 8], P('section'), may hold values from -0.078125 to 0.078125
- norm_gain: float32 [8, 6144], P('section'), may hold values from 0.1 to 1.9
Outputs:
- act_out: bfloat16 [8, 2048, 6144], P('section', 'expert')
- grad_out: bfloat16 [8, 2048, 6144], P('section', 'expert')
The draws below stay inside these ranges and needn't reach their ends.
Inputs may be any that keep to these rules, and one draw needn't show every extreme that they name: `fwd_routes`: per section, the 128 rows of one device name expert 0 between 16 and 32 times, and in every section some device's rows name it exactly 32 times; a token's two experts differ. `bwd_routes`: per section, the 128 rows of one device name expert 0 between 16 and 32 times, and in every section some device's rows name it exactly 32 times; a token's two experts differ.
All inputs are finite; a program needn't handle non-finite values.
Results may differ from the reference program's by a relative error of at most 0.007.
Values may be sent and summed in bfloat16 or wider, within the bound.
A program may use at most 128 MiB of HBM per device.

```python
import jax
import jax.numpy as jnp
from jax import lax

D = 6144
EXPERTS = 8
HID = 8192
TOK_DEV = 128
SECTIONS = 8
TOKENS = 2048
CAP = 32
N_EXPERT = 16


def window_routes(key):
    keys = jax.random.split(key, 6)
    blocks = SECTIONS * N_EXPERT
    counts = jax.random.randint(keys[0], (blocks,), CAP // 2, CAP + 1)
    forced = jax.random.randint(keys[1], (SECTIONS,), 0, N_EXPERT)
    block_ids = jnp.arange(blocks, dtype=jnp.int32)
    counts = jnp.where(block_ids % N_EXPERT == forced[block_ids // N_EXPERT], CAP, counts)
    shuffled = jax.vmap(lambda subkey: jax.random.permutation(subkey, TOK_DEV))(jax.random.split(keys[2], blocks))
    rank_in = jnp.argsort(shuffled, axis=1, stable=True)
    has_zero = rank_in < counts[:, None]
    first_pick = jax.random.randint(keys[3], (blocks, TOK_DEV), 1, EXPERTS)
    second_pick = jax.random.randint(keys[4], (blocks, TOK_DEV), 1, EXPERTS - 1)
    second_pick = second_pick + (second_pick >= first_pick).astype(jnp.int32)
    which_side = jax.random.randint(keys[5], (blocks, TOK_DEV), 0, 2)
    one_id = jnp.where(has_zero, jnp.where(which_side == 0, 0, first_pick), first_pick)
    two_id = jnp.where(has_zero, jnp.where(which_side == 0, first_pick, 0), second_pick)
    return jnp.stack([one_id, two_id], axis=2).reshape(SECTIONS, TOKENS, 2).astype(jnp.int32)


def draw_fwd_routes(key, part):
    return window_routes(jax.random.fold_in(key, 11))


def draw_bwd_routes(key, part):
    return window_routes(jax.random.fold_in(key, 23))


def shard_levels(own_key, shape, cuts, low, largest):
    def one(axis_at, parts):
        steps = jax.random.uniform(jax.random.fold_in(jax.random.fold_in(own_key, 6), axis_at), (parts,), jnp.float32, low / len(cuts), largest / len(cuts))
        return jnp.repeat(jnp.exp(steps), shape[axis_at] // parts).reshape((-1,) + (1,) * (len(shape) - axis_at - 1))

    loudness = one(*cuts[0])
    for cut in cuts[1:]:
        loudness = loudness * one(*cut)
    return loudness


def noise(own_key, extent, spread, limit, pieces=(), kind=jnp.bfloat16):
    loudness = shard_levels(own_key, extent, pieces, -0.22, 0.18) if pieces else 1.0
    entries = jax.random.normal(own_key, extent, jnp.float32) * spread * loudness
    return jnp.minimum(jnp.maximum(entries, -limit), limit).astype(kind)


def setup_inputs(seed: int = 0) -> dict:
    arg_keys = jax.random.split(jax.random.key(seed), 11)
    act_in = noise(arg_keys[0], (SECTIONS, TOKENS, D), 1.0, 6.0, ((0, 8), (1, 16)))
    saved_in = noise(arg_keys[1], (SECTIONS, TOKENS, D), 1.0, 6.0, ((0, 8), (1, 16)))
    grad_in = noise(arg_keys[2], (SECTIONS, TOKENS, D), 1.0, 6.0, ((0, 8), (1, 16)))
    fwd_routes = draw_fwd_routes(jax.random.fold_in(arg_keys[10], 71), 0)
    bwd_routes = draw_bwd_routes(jax.random.fold_in(arg_keys[10], 71), 0)
    w_gate = noise(arg_keys[5], (SECTIONS, D, HID), D ** -0.5, 0.078125, ((0, 8), (2, 16)))
    w_up = noise(arg_keys[6], (SECTIONS, D, HID), D ** -0.5, 0.078125, ((0, 8), (2, 16)))
    w_down = noise(arg_keys[7], (SECTIONS, HID, D), HID ** -0.5, 0.0625, ((0, 8), (1, 16)))
    router = noise(arg_keys[8], (SECTIONS, D, EXPERTS), D ** -0.5, 0.078125, ((0, 8),), jnp.float32)
    norm_gain = jnp.clip(1.0 + 0.18 * jax.random.normal(arg_keys[9], (SECTIONS, D), jnp.float32), 0.1, 1.9)
    return {"act_in": act_in, "saved_in": saved_in, "grad_in": grad_in, "fwd_routes": fwd_routes, "bwd_routes": bwd_routes, "w_gate": w_gate, "w_up": w_up, "w_down": w_down, "router": router, "norm_gain": norm_gain}


epsilon = 1e-05
highest = lax.Precision.HIGHEST

def norm_route(inputs, gain_row, router_mat, chosen_ids):
    inverse = lax.rsqrt(lax.optimization_barrier(jnp.mean(inputs * inputs, axis=1, keepdims=True)) + epsilon)
    normed = inputs * inverse * gain_row[None, :]
    logits = jnp.dot(normed, router_mat, precision=highest)
    onehot = (chosen_ids[:, :, None] == jnp.arange(router_mat.shape[1], dtype=jnp.int32)[None, None, :]).astype(jnp.float32)
    picked = lax.optimization_barrier(jnp.sum(onehot * logits[:, None, :], axis=2))
    first_share = jax.nn.sigmoid(picked[:, 0] - picked[:, 1])
    shares = jnp.stack([first_share, 1.0 - first_share], axis=1)
    window_weight = lax.optimization_barrier(jnp.sum(shares * (chosen_ids == 0).astype(jnp.float32), axis=1))
    return (normed, window_weight)

def assign_window(chosen_ids, capacity):
    named_zero = lax.optimization_barrier(jnp.sum((chosen_ids == 0).astype(jnp.int32), axis=1))
    rank_in = jnp.cumsum(named_zero) - named_zero
    slot_of = jnp.where(named_zero > 0, rank_in, capacity).astype(jnp.int32)
    matches = (slot_of[None, :] == jnp.arange(capacity, dtype=jnp.int32)[:, None]).astype(jnp.int32)
    token_ids = jnp.arange(chosen_ids.shape[0], dtype=jnp.int32) + 1
    source = (lax.optimization_barrier(jnp.sum(matches * token_ids[None, :], axis=1)) - 1).astype(jnp.int32)
    return (slot_of, source)

def fill_rows(values, source):
    picked = jnp.take(values, jnp.maximum(source, 0), axis=0)
    keep = (source >= 0).reshape((-1,) + (1,) * (values.ndim - 1))
    return jnp.where(keep, picked, jnp.zeros_like(picked))

def unfill(lookup, slot_of):
    padded = jnp.concatenate([lookup, jnp.zeros((1,) + lookup.shape[1:], lookup.dtype)], axis=0)
    return jnp.take(padded, slot_of, axis=0)

def forward_part(slot_rows, gate_cols, up_cols, down_rows):
    gate_pre = jnp.dot(slot_rows, gate_cols, preferred_element_type=jnp.float32)
    up_pre = jnp.dot(slot_rows, up_cols, preferred_element_type=jnp.float32)
    active = (gate_pre * jax.nn.sigmoid(gate_pre) * up_pre).astype(jnp.bfloat16)
    return jnp.dot(active, down_rows, preferred_element_type=jnp.float32).astype(jnp.bfloat16)

def backward_part(slot_rows, upstream_rows, weight_col, gate_cols, up_cols, down_rows):
    last_dims = (((1,), (1,)), ((), ()))
    gate_pre = jnp.dot(slot_rows, gate_cols, preferred_element_type=jnp.float32)
    up_pre = jnp.dot(slot_rows, up_cols, preferred_element_type=jnp.float32)
    gate_sig = jax.nn.sigmoid(gate_pre)
    silu_val = gate_pre * gate_sig
    active = (silu_val * up_pre).astype(jnp.bfloat16)
    back_cols = lax.dot_general(upstream_rows, down_rows, last_dims, preferred_element_type=jnp.float32)
    slope_part = lax.optimization_barrier(jnp.sum(active.astype(jnp.float32) * back_cols, axis=1)).astype(jnp.bfloat16)
    act_cot = weight_col[:, None] * back_cols
    gate_cot = (act_cot * up_pre * gate_sig * (1.0 + gate_pre * (1.0 - gate_sig))).astype(jnp.bfloat16)
    up_cot = (act_cot * silu_val).astype(jnp.bfloat16)
    row_part = (lax.dot_general(gate_cot, gate_cols, last_dims, preferred_element_type=jnp.float32) + lax.dot_general(up_cot, up_cols, last_dims, preferred_element_type=jnp.float32)).astype(jnp.bfloat16)
    return (row_part, slope_part)

def reference(act_in, saved_in, grad_in, fwd_routes, bwd_routes, w_gate, w_up, w_down, router, norm_gain):
    hid_dev = HID // N_EXPERT
    slot_total = N_EXPERT * CAP

    def assign(chosen_ids):
        return assign_window(chosen_ids, CAP)

    def one_section(section_pos):
        gate_all = lax.dynamic_index_in_dim(w_gate, section_pos, 0, keepdims=False)
        up_all = lax.dynamic_index_in_dim(w_up, section_pos, 0, keepdims=False)
        down_all = lax.dynamic_index_in_dim(w_down, section_pos, 0, keepdims=False)
        router_mat = lax.dynamic_index_in_dim(router, section_pos, 0, keepdims=False)
        gain_row = lax.dynamic_index_in_dim(norm_gain, section_pos, 0, keepdims=False)
        fwd_x = lax.dynamic_index_in_dim(act_in, section_pos, 0, keepdims=False).astype(jnp.float32)
        fwd_ids = lax.dynamic_index_in_dim(fwd_routes, section_pos, 0, keepdims=False)
        normed_f, weight_f = norm_route(fwd_x, gain_row, router_mat, fwd_ids)
        slot_f, source_f = jax.vmap(assign)(fwd_ids.reshape(N_EXPERT, TOK_DEV, 2))
        rows_f = jax.vmap(fill_rows)(normed_f.astype(jnp.bfloat16).reshape(N_EXPERT, TOK_DEV, D), source_f)
        rows_f = rows_f.reshape(slot_total, D)
        back_x = lax.dynamic_index_in_dim(saved_in, section_pos, 0, keepdims=False).astype(jnp.float32)
        upstream = lax.dynamic_index_in_dim(grad_in, section_pos, 0, keepdims=False)
        bwd_ids = lax.dynamic_index_in_dim(bwd_routes, section_pos, 0, keepdims=False)

        def front(inputs):
            return norm_route(inputs, gain_row, router_mat, bwd_ids)
        (normed_b, weight_b), pullback = jax.vjp(front, back_x)
        slot_b, source_b = jax.vmap(assign)(bwd_ids.reshape(N_EXPERT, TOK_DEV, 2))
        rows_h = jax.vmap(fill_rows)(normed_b.astype(jnp.bfloat16).reshape(N_EXPERT, TOK_DEV, D), source_b)
        rows_u = jax.vmap(fill_rows)(upstream.reshape(N_EXPERT, TOK_DEV, D), source_b)
        rows_q = jax.vmap(fill_rows)(weight_b.astype(jnp.bfloat16).reshape(N_EXPERT, TOK_DEV), source_b)
        rows_h = rows_h.reshape(slot_total, D)
        rows_u = rows_u.reshape(slot_total, D)
        weight_col = rows_q.reshape(slot_total).astype(jnp.float32)

        def add_slice(slice_pos, running):
            first_col = (slice_pos * hid_dev).astype(jnp.int32)
            gate_cols = lax.dynamic_slice_in_dim(gate_all, first_col, hid_dev, 1)
            up_cols = lax.dynamic_slice_in_dim(up_all, first_col, hid_dev, 1)
            down_rows = lax.dynamic_slice_in_dim(down_all, first_col, hid_dev, 0)
            out_part = forward_part(rows_f, gate_cols, up_cols, down_rows)
            row_part, slope_part = backward_part(rows_h, rows_u, weight_col, gate_cols, up_cols, down_rows)
            return (running[0] + out_part.astype(jnp.float32), running[1] + row_part.astype(jnp.float32), running[2] + slope_part.astype(jnp.float32))
        initial = (jnp.zeros((slot_total, D), jnp.float32), jnp.zeros((slot_total, D), jnp.float32), jnp.zeros((slot_total,), jnp.float32))
        expert_out, row_cot, slope_sum = lax.fori_loop(0, N_EXPERT, add_slice, initial)
        picked_f = jax.vmap(unfill)(expert_out.reshape(N_EXPERT, CAP, D), slot_f).reshape(TOKENS, D)
        layer_out = (fwd_x + weight_f[:, None] * picked_f).astype(jnp.bfloat16)
        cot_normed = jax.vmap(unfill)(row_cot.reshape(N_EXPERT, CAP, D), slot_b).reshape(TOKENS, D)
        cot_weight = jax.vmap(unfill)(slope_sum.reshape(N_EXPERT, CAP), slot_b).reshape(TOKENS)
        d_rows = pullback((cot_normed, cot_weight))[0]
        grad_rows = (upstream.astype(jnp.float32) + d_rows).astype(jnp.bfloat16)
        return (layer_out, grad_rows)
    results = lax.map(one_section, jnp.arange(SECTIONS, dtype=jnp.int32))
    act_out = jnp.roll(results[0], 1, axis=0)
    grad_out = jnp.roll(results[1], -1, axis=0)
    return (act_out, grad_out)
```

```python
import functools

import jax
import jax.numpy as jnp
from jax import lax
from jax.experimental import pallas as pl
from jax.experimental.pallas import tpu as pltpu
from jax.sharding import PartitionSpec as P

EPS = 1e-05
NC = 6
CAP = 32
NS = 4
LEAD = 3
F32 = jnp.float32
BF16 = jnp.bfloat16
MESH = pl.DeviceIdType.MESH
HI = lax.Precision.HIGHEST
LAST = (((1,), (1,)), ((), ()))


def chosen(routes_t):
    tok = routes_t.shape[1]
    named = jnp.max((routes_t == 0).astype(F32), axis=0, keepdims=True)
    before = lax.broadcasted_iota(jnp.int32, (tok, tok), 0) < lax.broadcasted_iota(jnp.int32, (tok, tok), 1)
    wide = jnp.broadcast_to(named, (8, tok)).astype(BF16)
    rank = jnp.dot(wide, before.astype(F32).astype(BF16), preferred_element_type=F32)[0:1]
    slot = lax.broadcasted_iota(jnp.int32, (CAP, tok), 0).astype(F32)
    return jnp.where((slot == rank) & (named > 0.5), 1.0, 0.0).astype(BF16)


def prologue_kernel(act, saved, grad, rt_f, rt_b, router_t, gain, send, xf, xb, stats):
    width = send.shape[-1]
    depth = act.shape[1]

    def pick(onehot, source, c):
        return jnp.dot(onehot, source[:, c * width:(c + 1) * width], preferred_element_type=F32)

    def halves(value):
        return value.reshape(2, 16, width)

    def experts(onehot, routes):
        wide = jnp.concatenate([routes[...].astype(F32), jnp.zeros((6, routes.shape[1]), F32)], axis=0)
        both = lax.dot_general(onehot, wide.astype(BF16), LAST, preferred_element_type=F32)
        return both[:, 0:1], both[:, 1:2]

    pick_f = chosen(rt_f[...])
    pick_b = chosen(rt_b[...])
    for c in range(NC):
        send[c] = halves(pick(pick_b, grad, c).astype(BF16))

    def route(onehot, source, rows, routes, base):
        total = jnp.zeros((CAP, 1), F32)
        for c in range(NC):
            x = pick(onehot, source, c)
            rows[c] = halves(x.astype(BF16))
            total = total + jnp.sum(x * x, axis=1, keepdims=True)
        inverse = lax.rsqrt(total / depth + EPS)
        logits = jnp.zeros((CAP, 8), F32)
        for c in range(NC):
            cols = slice(c * width, (c + 1) * width)
            normed = rows[c].reshape(CAP, width).astype(F32) * inverse * gain[:, cols]
            send[base + c] = halves(normed.astype(BF16))
            logits = logits + lax.dot_general(
                normed, router_t[:, cols], LAST, precision=HI, preferred_element_type=F32
            )
        first, second = experts(onehot, routes)
        ids = lax.broadcasted_iota(jnp.int32, (CAP, 8), 1).astype(F32)
        picked1 = jnp.sum(jnp.where(ids == first, logits, 0.0), axis=1, keepdims=True)
        picked2 = jnp.sum(jnp.where(ids == second, logits, 0.0), axis=1, keepdims=True)
        share = jax.nn.sigmoid(picked1 - picked2)
        on1 = jnp.where(first == 0.0, 1.0, 0.0)
        on2 = jnp.where(second == 0.0, 1.0, 0.0)
        weight = share * on1 + (1.0 - share) * on2
        slope_scale = (on1 - on2) * share * (1.0 - share)
        return weight, inverse, slope_scale, first, second

    weight_f = route(pick_f, act, xf, rt_f, NC)[0]
    weight_b, inv_b, scale_b, first_b, second_b = route(pick_b, saved, xb, rt_b, 2 * NC)
    lane = lax.broadcasted_iota(jnp.int32, (CAP, 128), 1)
    table = jnp.zeros((CAP, 128), F32)
    for k, col in enumerate(
        (weight_f, weight_b.astype(BF16).astype(F32), inv_b, scale_b, first_b, second_b)
    ):
        table = jnp.where(lane == k, col, table)
    stats[...] = table


def main_kernel(
    send, xf, xb, stats, router_t, gain, rt_f, rt_b, act, grad, w_gate, w_up, w_down,
    rows_f, rows_b, rt_f2, rt_b2, act2, grad2,
    gath, gw, uw, dw, gacc, uacc, bacc, activ, gcot, ucot,
    part, r1, r2, q, r3, r4, gd, newf, newb, dots, slope, slope_in,
    ag_s1, ag_r1, ag_s, ag_r, rs_s, rs_r, sl_s, sl_r, w_sem, pass_s, pass_r, row_s, row_r,
):
    width = send.shape[-1]
    half_w = width // 2
    hid = gacc.shape[1]
    rows = gacc.shape[0]
    depth = gain.shape[1]
    n_ag, n_rs = 3 * NC, 2 * NC
    t_rs = n_ag
    n_sec = lax.axis_size("section")

    sec = lax.axis_index("section")
    ex = lax.axis_index("expert")
    y, z = ex // 4, ex % 4

    def turn(v, k):
        return (v + k + 4) % 4

    def dev_y(d):
        return (sec, turn(y, d) * 4 + z)

    def dev_z(d):
        return (sec, y * 4 + turn(z, d))

    sec_next = ((sec + 1) % n_sec, ex)
    sec_prev = ((sec + n_sec - 1) % n_sec, ex)
    DIRS = (1, -1)

    barrier = pltpu.get_barrier_semaphore()
    for dev in (dev_y(1), dev_y(-1), dev_z(1), dev_z(-1), sec_next, sec_prev):
        pl.semaphore_signal(barrier, inc=1, device_id=dev, device_id_type=MESH)

    def weight_copies(c):
        span = pl.ds(c * width, width)
        return (
            pltpu.make_async_copy(w_down.at[:, span], dw.at[c], w_sem.at[0, c]),
            pltpu.make_async_copy(w_gate.at[span, :], gw.at[c], w_sem.at[1, c]),
            pltpu.make_async_copy(w_up.at[span, :], uw.at[c], w_sem.at[2, c]),
        )

    own = pltpu.make_async_copy(send, gath.at[:, y, z], w_sem.at[3, 0])
    own.start()
    for c in range(NC):
        weight_copies(c)[0].start()
    for c in range(NC):
        weight_copies(c)[1].start()
        weight_copies(c)[2].start()

    def msg(src, dst, arrive, ssem, rsem, dev):
        def copy(target):
            return pltpu.make_async_remote_copy(
                src_ref=src, dst_ref=target, send_sem=ssem, recv_sem=rsem,
                device_id=dev, device_id_type=MESH,
            )

        def start():
            copy(dst).start()

        def finish():
            done = copy(arrive)
            done.wait_send()
            done.wait_recv()

        return start, finish

    def start_all(messages):
        for start, _ in messages:
            start()

    def finish_all(messages):
        for _, finish in messages:
            finish()

    COLS = (slice(0, half_w), slice(half_w, width))
    PAIR = (slice(0, 2), slice(2, 4))
    ALL = slice(0, 4)

    def ag_pos(h):
        return ((y, z, dev_y, dev_z), (z, y, dev_z, dev_y))[h]

    def g_at(n, fa, sa, h):
        return gath.at[n, fa, sa, h] if h == 0 else gath.at[n, sa, fa, h]

    def g_cols(n, fa, sa, h, cols):
        if h == 0:
            return gath.at[n, fa, sa, h, :, cols]
        return gath.at[n, sa, fa, h, :, cols]

    def ag1(n):
        out = []
        slot = n % 8
        for h in range(2):
            f, s, first, _ = ag_pos(h)
            for i, d in enumerate(DIRS):
                out.append(msg(send.at[n, h], g_at(n, f, s, h), g_at(n, turn(f, -d), s, h),
                               ag_s1.at[h, i, slot], ag_r1.at[h, i, slot], first(d)))
        return out

    def ag2(n):
        out = []
        slot = n % NS
        for h in range(2):
            f, s, first, _ = ag_pos(h)
            for i, d in enumerate(DIRS):
                src = g_cols(n, turn(f, -d), s, h, COLS[i])
                out.append(msg(src, src, g_cols(n, turn(f, 2), s, h, COLS[i]),
                               ag_s.at[0, h, i, slot], ag_r.at[0, h, i, slot], first(d)))
        return out

    def ag3(n):
        out = []
        slot = n % NS
        for h in range(2):
            f, s, _, second = ag_pos(h)
            for i, d in enumerate(DIRS):
                src = g_at(n, ALL, s, h)
                out.append(msg(src, src, g_at(n, ALL, turn(s, -d), h),
                               ag_s.at[1, h, i, slot], ag_r.at[1, h, i, slot], second(d)))
        return out

    def ag4(n):
        out = []
        slot = n % NS
        for h in range(2):
            f, s, _, second = ag_pos(h)
            for i, d in enumerate(DIRS):
                src = g_at(n, PAIR[i], turn(s, -d), h)
                out.append(msg(src, src, g_at(n, PAIR[i], turn(s, 2), h),
                               ag_s.at[2, h, i, slot], ag_r.at[2, h, i, slot], second(d)))
        return out

    def rs_pos(h):
        return ((z, y, dev_z, dev_y), (y, z, dev_y, dev_z))[h]

    def p_idx(slot, fa, sa, h):
        return (slot, sa, fa, h) if h == 0 else (slot, fa, sa, h)

    def rs1(m):
        out = []
        slot = m % NS
        for h in range(2):
            f, s, first, _ = rs_pos(h)
            for i, d in enumerate(DIRS):
                into = r1.at[h, i, slot]
                out.append(msg(part.at[p_idx(slot, turn(f, 2), PAIR[i], h)], into, into,
                               rs_s.at[0, h, i, slot], rs_r.at[0, h, i, slot], first(d)))
        return out

    def rs2(m):
        out = []
        slot = m % NS
        for h in range(2):
            f, s, first, _ = rs_pos(h)
            for i, d in enumerate(DIRS):
                into = r2.at[h, i, slot]
                out.append(msg(part.at[p_idx(slot, turn(f, d), ALL, h)], into, into,
                               rs_s.at[1, h, i, slot], rs_r.at[1, h, i, slot], first(d)))
        return out

    def rs3(m):
        out = []
        slot = m % NS
        for h in range(2):
            f, s, _, second = rs_pos(h)
            for i, d in enumerate(DIRS):
                into = r3.at[h, i, slot]
                out.append(msg(q.at[h, slot, turn(s, 2), :, COLS[i]], into, into,
                               rs_s.at[2, h, i, slot], rs_r.at[2, h, i, slot], second(d)))
        return out

    def rs4(m):
        out = []
        slot = m % NS
        for h in range(2):
            f, s, _, second = rs_pos(h)
            for i, d in enumerate(DIRS):
                into = r4.at[h, i, slot]
                out.append(msg(q.at[h, slot, turn(s, d)], into, into,
                               rs_s.at[3, h, i, slot], rs_r.at[3, h, i, slot], second(d)))
        return out

    def add1(m):
        slot = m % NS
        for h in range(2):
            f = rs_pos(h)[0]
            for i, d in enumerate(DIRS):
                at = p_idx(slot, turn(f, d), PAIR[i], h)
                part[at] = (part[at].astype(F32) + r1[h, i, slot].astype(F32)).astype(BF16)

    def add2(m):
        slot = m % NS
        for h in range(2):
            f = rs_pos(h)[0]
            mine = part[p_idx(slot, f, ALL, h)].astype(F32)
            q[h, slot] = (mine + r2[h, 0, slot].astype(F32) + r2[h, 1, slot].astype(F32)).astype(BF16)

    def add3(m):
        slot = m % NS
        for h in range(2):
            s = rs_pos(h)[1]
            for i, d in enumerate(DIRS):
                to = turn(s, d)
                q[h, slot, to, :, COLS[i]] = (
                    q[h, slot, to, :, COLS[i]].astype(F32) + r3[h, i, slot].astype(F32)
                ).astype(BF16)

    def summed(m, h):
        slot = m % NS
        s = rs_pos(h)[1]
        return (
            q[h, slot, s].astype(F32) + r4[h, 0, slot].astype(F32) + r4[h, 1, slot].astype(F32)
        )

    def sl_msgs(k, stage):
        axis_dev = (dev_z, dev_y)[k]
        if stage == 0:
            return [
                msg(slope.at[k], slope_in.at[k, i], slope_in.at[k, i],
                    sl_s.at[k, i], sl_r.at[k, i], axis_dev(d))
                for i, d in enumerate(DIRS)
            ]
        return [
            msg(slope_in.at[k, 0], slope_in.at[k, 2], slope_in.at[k, 2],
                sl_s.at[k, 2], sl_r.at[k, 2], axis_dev(1))
        ]

    def sl_sum(k):
        slope[k + 1] = slope[k] + slope_in[k, 0] + slope_in[k, 1] + slope_in[k, 2]

    def pass_msgs():
        out = []
        for i, (src, dst, dev) in enumerate(
            ((act, act2, sec_next), (grad, grad2, sec_prev), (rt_f, rt_f2, sec_next), (rt_b, rt_b2, sec_prev))
        ):
            out.append(msg(src, dst, dst, pass_s.at[i], pass_r.at[i], dev))
        return out

    row_f_msg = msg(newf, rows_f, rows_f, row_s.at[NC], row_r.at[NC], sec_next)

    def row_b_msg(c):
        return msg(newb.at[c], rows_b.at[c], rows_b.at[c], row_s.at[c], row_r.at[c], sec_prev)

    def lhs(n):
        return gath[n].reshape(rows, width)

    def fwd_rows(i, _):
        span = pl.ds(i * 64, 64)
        g = gacc[span, :]
        activ[span, :] = (g * jax.nn.sigmoid(g) * uacc[span, :]).astype(BF16)
        gacc[span, :] = jnp.zeros((64, hid), F32)
        uacc[span, :] = jnp.zeros((64, hid), F32)
        return 0

    def bwd_rows(i, _):
        span = pl.ds(i * 128, 128)
        g = gacc[span, :]
        u = uacc[span, :]
        back = bacc[span, :]
        sig = jax.nn.sigmoid(g)
        silu = g * sig
        prod = (silu * u).astype(BF16).astype(F32) * back
        high = prod.astype(BF16)
        low = (prod - high.astype(F32)).astype(BF16)
        ones = jnp.ones((8, hid), BF16)
        slope[0, :, span] = lax.dot_general(
            ones, high, LAST, preferred_element_type=F32
        ) + lax.dot_general(ones, low, LAST, preferred_element_type=F32)
        gcot[span, :] = (back * u * sig * (1.0 + g * (1.0 - sig))).astype(BF16)
        ucot[span, :] = (back * silu).astype(BF16)
        return 0

    def col(h, k):
        return stats[h * 16:(h + 1) * 16, k:k + 1]

    def finish_forward(m):
        for h in range(2):
            newf[m, h] = (xf[m, h].astype(F32) + col(h, 0) * summed(m, h)).astype(BF16)

    def finish_backward(m):
        c = m - NC
        span = pl.ds(pl.multiple_of(c * width, 128), width)
        router_c = router_t[:, span]
        gain_c = gain[:, span]
        ids = lax.broadcasted_iota(jnp.int32, (16, 8), 1).astype(F32)
        place = lax.broadcasted_iota(jnp.int32, (16, rows), 1)
        row = lax.broadcasted_iota(jnp.int32, (16, rows), 0)
        for h in range(2):
            mine = place == row + (ex * CAP + h * 16)
            cot = jnp.sum(jnp.where(mine, slope[2, 0:1, :], 0.0), axis=1, keepdims=True) * col(h, 3)
            both = jnp.where(ids == col(h, 4), 1.0, 0.0) - jnp.where(ids == col(h, 5), 1.0, 0.0)
            dlog = cot * both
            dn = col(h, 1) * summed(m, h)
            for e in range(8):
                dn = dn + dlog[:, e:e + 1] * router_c[e:e + 1, :]
            dn = dn * gain_c
            gd[c, h] = dn
            line = jnp.sum(dn * xb[c, h].astype(F32), axis=1, keepdims=True)
            at = slice(h * 16, (h + 1) * 16)
            dots[at, :] = dots[at, :] + jnp.broadcast_to(line, (16, 128))

    gacc[...] = jnp.zeros_like(gacc)
    uacc[...] = jnp.zeros_like(uacc)
    bacc[...] = jnp.zeros_like(bacc)
    dots[...] = jnp.zeros_like(dots)

    pl.semaphore_wait(barrier, 6)
    for n in range(LEAD):
        start_all(ag1(n))
    start_all(pass_msgs())
    own.wait()

    def when_in(value, low, high):
        return pl.when(jnp.logical_and(value >= low, value < high))

    def step(t, _):
        @when_in(t, 0, n_ag - LEAD)
        def _():
            start_all(ag1(t + LEAD))

        @when_in(t, 1, n_ag + 1)
        def _():
            finish_all(ag1(t - 1))
            start_all(ag2(t - 1))

        @when_in(t, 2, n_ag + 2)
        def _():
            finish_all(ag2(t - 2))
            start_all(ag3(t - 2))

        @when_in(t, 3, n_ag + 3)
        def _():
            finish_all(ag3(t - 3))
            start_all(ag4(t - 3))

        @when_in(t, 4, n_ag + 4)
        def _():
            finish_all(ag4(t - 4))

        r = t - t_rs

        @when_in(r, 0, n_rs)
        def _():
            start_all(rs1(r))

        @when_in(r, 1, n_rs + 1)
        def _():
            finish_all(rs1(r - 1))
            add1(r - 1)
            start_all(rs2(r - 1))

        @when_in(r, 2, n_rs + 2)
        def _():
            finish_all(rs2(r - 2))
            add2(r - 2)
            start_all(rs3(r - 2))

        @when_in(r, 3, n_rs + 3)
        def _():
            finish_all(rs3(r - 3))
            add3(r - 3)
            start_all(rs4(r - 3))

        @when_in(r, 4, n_rs + 4)
        def _():
            finish_all(rs4(r - 4))

        @when_in(r, 4, NC + 4)
        def _():
            finish_forward(r - 4)

        @pl.when(r == NC + 3)
        def _():
            row_f_msg[0]()

        @pl.when(t == n_ag + 4)
        def _():
            start_all(sl_msgs(0, 0))

        @pl.when(t == n_ag + 5)
        def _():
            finish_all(sl_msgs(0, 0))
            start_all(sl_msgs(0, 1))

        @pl.when(t == n_ag + 6)
        def _():
            finish_all(sl_msgs(0, 1))
            sl_sum(0)
            start_all(sl_msgs(1, 0))

        @pl.when(t == n_ag + 7)
        def _():
            finish_all(sl_msgs(1, 0))
            start_all(sl_msgs(1, 1))

        @pl.when(t == n_ag + 8)
        def _():
            finish_all(sl_msgs(1, 1))
            sl_sum(1)

        @when_in(r, NC + 4, n_rs + 4)
        def _():
            finish_backward(r - 4)

        n = t - 4

        @when_in(n, 0, NC)
        def _():
            weight_copies(n)[0].wait()
            bacc[...] += lax.dot_general(lhs(n), dw[n], LAST, preferred_element_type=F32)

        @when_in(n, NC, 2 * NC)
        def _():
            weight_copies(n - NC)[1].wait()
            weight_copies(n - NC)[2].wait()

        @when_in(n, NC, n_ag)
        def _():
            c = n % NC
            gacc[...] += jnp.dot(lhs(n), gw[c], preferred_element_type=F32)
            uacc[...] += jnp.dot(lhs(n), uw[c], preferred_element_type=F32)

        @pl.when(n == 2 * NC - 1)
        def _():
            lax.fori_loop(0, rows // 64, fwd_rows, 0)

        @pl.when(n == n_ag - 1)
        def _():
            lax.fori_loop(0, rows // 128, bwd_rows, 0)

        m = r + 1
        shape = part.shape[1:]

        @when_in(m, 0, NC)
        def _():
            part[m % NS] = jnp.dot(activ[...], dw[m], preferred_element_type=F32).astype(BF16).reshape(shape)

        @when_in(m, NC, n_rs)
        def _():
            c = m - NC
            value = lax.dot_general(gcot[...], gw[c], LAST, preferred_element_type=F32)
            value = value + lax.dot_general(ucot[...], uw[c], LAST, preferred_element_type=F32)
            part[m % NS] = value.astype(BF16).reshape(shape)

        return 0

    lax.fori_loop(0, t_rs + n_rs + 4, step, 0)

    def last(c, _):
        for h in range(2):
            inv = col(h, 2)
            coef = inv * inv * inv * dots[h * 16:(h + 1) * 16, 0:1] / depth
            change = inv * gd[c, h] - coef * xb[c, h].astype(F32)
            newb[c, h] = (send[c, h].astype(F32) + change).astype(BF16)
        row_b_msg(c)[0]()
        return 0

    lax.fori_loop(0, NC, last, 0)

    finish_all(pass_msgs())
    row_f_msg[1]()

    def drain(c, _):
        row_b_msg(c)[1]()
        return 0

    lax.fori_loop(0, NC, drain, 0)


def merge_kernel(rt_f, rt_b, act, grad, rows_f, rows_b, out_f, out_b):
    width = act.shape[-1]
    for routes, plain, rows, out in ((rt_f, act, rows_f, out_f), (rt_b, grad, rows_b, out_b)):
        onehot = chosen(routes[...])
        first = (((0,), (0,)), ((), ()))
        moved = lax.dot_general(onehot, rows[0].reshape(CAP, width), first, preferred_element_type=F32)
        held = lax.dot_general(onehot, jnp.ones((CAP, 128), BF16), first, preferred_element_type=F32)
        out[...] = jnp.where(held[:, 0:1] > 0.5, moved, plain[...].astype(F32)).astype(BF16)


def local(act_in, saved_in, grad_in, fwd_routes, bwd_routes, w_gate, w_up, w_down, router, norm_gain):
    act, saved, grad = act_in[0], saved_in[0], grad_in[0]
    rt_f, rt_b = fwd_routes[0].T, bwd_routes[0].T
    router_t = router[0].T
    tok, depth = act.shape
    width = depth // NC
    hid = w_gate.shape[2]
    rows = 16 * CAP
    sds = jax.ShapeDtypeStruct
    vmem = pl.BlockSpec(memory_space=pltpu.VMEM)
    anywhere = pl.BlockSpec(memory_space=pl.ANY)
    dma = pltpu.SemaphoreType.DMA
    row_shape = (NC, 2, 16, width)

    send, xf, xb, stats = pl.pallas_call(
        prologue_kernel,
        out_shape=(
            sds((3 * NC, 2, 16, width), BF16), sds(row_shape, BF16), sds(row_shape, BF16), sds((CAP, 128), F32),
        ),
        in_specs=[vmem] * 7,
        out_specs=(vmem,) * 4,
        compiler_params=pltpu.CompilerParams(vmem_limit_bytes=32 << 20),
    )(act, saved, grad, rt_f, rt_b, router_t, norm_gain)

    V = pltpu.VMEM
    rows_f, rows_b, rt_f2, rt_b2, act2, grad2 = pl.pallas_call(
        main_kernel,
        out_shape=(
            sds(row_shape, BF16), sds(row_shape, BF16),
            sds(rt_f.shape, jnp.int32), sds(rt_b.shape, jnp.int32),
            sds(act.shape, BF16), sds(grad.shape, BF16),
        ),
        in_specs=[vmem] * 8 + [anywhere] * 5,
        out_specs=(vmem,) * 4 + (anywhere,) * 2,
        scratch_shapes=[
            V((3 * NC, 4, 4, 2, 16, width), BF16),
            V((NC, width, hid), BF16), V((NC, width, hid), BF16), V((NC, hid, width), BF16),
            V((rows, hid), F32), V((rows, hid), F32), V((rows, hid), F32),
            V((rows, hid), BF16), V((rows, hid), BF16), V((rows, hid), BF16),
            V((NS, 4, 4, 2, 16, width), BF16),
            V((2, 2, NS, 2, 16, width), BF16), V((2, 2, NS, 4, 16, width), BF16),
            V((2, NS, 4, 16, width), BF16),
            V((2, 2, NS, 16, width // 2), BF16), V((2, 2, NS, 16, width), BF16),
            V(row_shape, F32), V(row_shape, BF16), V(row_shape, BF16), V((CAP, 128), F32),
            V((3, 8, rows), F32), V((2, 3, 8, rows), F32),
            dma((2, 2, 8)), dma((2, 2, 8)),
            dma((3, 2, 2, NS)), dma((3, 2, 2, NS)),
            dma((4, 2, 2, NS)), dma((4, 2, 2, NS)),
            dma((2, 3)), dma((2, 3)),
            dma((4, NC)), dma((4,)), dma((4,)), dma((NC + 1,)), dma((NC + 1,)),
        ],
        compiler_params=pltpu.CompilerParams(
            collective_id=0, has_side_effects=True, vmem_limit_bytes=67_000_000
        ),
    )(send, xf, xb, stats, router_t, norm_gain, rt_f, rt_b, act, grad, w_gate[0], w_up[0], w_down[0])

    whole = pl.BlockSpec(rt_f.shape, lambda c: (0, 0))
    columns = pl.BlockSpec((tok, width), lambda c: (0, c))
    slots = pl.BlockSpec((1, 2, 16, width), lambda c: (c, 0, 0, 0))
    out_f, out_b = pl.pallas_call(
        merge_kernel,
        grid=(NC,),
        out_shape=(sds(act.shape, BF16), sds(grad.shape, BF16)),
        in_specs=[whole, whole, columns, columns, slots, slots],
        out_specs=(columns, columns),
    )(rt_f2, rt_b2, act2, grad2, rows_f, rows_b)
    return (out_f[None], out_b[None])


def solution(mesh):
    in_specs = (
        P("section", "expert", None),
        P("section", "expert", None),
        P("section", "expert", None),
        P("section", "expert", None),
        P("section", "expert", None),
        P("section", None, "expert"),
        P("section", None, "expert"),
        P("section", "expert", None),
        P("section", None, None),
        P("section", None),
    )
    out_specs = (P("section", "expert", None), P("section", "expert", None))
    return jax.shard_map(local, mesh=mesh, in_specs=in_specs, out_specs=out_specs, check_vma=False)
```

```python
import functools

import jax
import jax.numpy as jnp
from jax import lax
from jax.experimental import pallas as pl
from jax.experimental.pallas import tpu as pltpu
from jax.sharding import PartitionSpec as P

EPS = 1e-05
NC = 4
MERGE = 2
CAP = 32
LAG = 2
NS = 2 * LAG + 1
NG = 8
F32 = jnp.float32
BF16 = jnp.bfloat16
MESH = pl.DeviceIdType.MESH
HI = lax.Precision.HIGHEST
LAST = (((1,), (1,)), ((), ()))


def chosen(routes_t):
    tok = routes_t.shape[1]
    named = jnp.max((routes_t == 0).astype(F32), axis=0, keepdims=True)
    before = lax.broadcasted_iota(jnp.int32, (tok, tok), 0) < lax.broadcasted_iota(jnp.int32, (tok, tok), 1)
    wide = jnp.broadcast_to(named, (8, tok)).astype(BF16)
    rank = jnp.dot(wide, before.astype(F32).astype(BF16), preferred_element_type=F32)[0:1]
    slot = lax.broadcasted_iota(jnp.int32, (CAP, tok), 0).astype(F32)
    onehot = jnp.where((slot == rank) & (named > 0.5), 1.0, 0.0).astype(BF16)
    return onehot, named


def main_kernel(
    act, saved, grad, rt_f, rt_b, router, norm_gain, w_gate, w_up, w_down,
    rows_f, rows_b, sel_f, sel_b, act2, grad2,
    source, routes, router_t, gain, xf, xb, stats, sel,
    gath, gw, uw, dw, gacc, uacc, bacc, activ, gcot, ucot,
    part, r1, r2, q, r3, r4, slope, slope_in,
    one_s, one_r, grp_s, grp_r, ag_s, ag_r, rs_s, rs_r, sl_s, sl_r,
    in_sem, small_sem, pass_s, pass_r, row_s, row_r,
):
    width = gath.shape[-1]
    half_w = width // 2
    hid = gacc.shape[1]
    rows = gacc.shape[0]
    depth = gain.shape[1]
    n_ag, n_rs = 3 * NC, 2 * NC
    t_rs = n_ag + 1
    n_sec = lax.axis_size("section")

    sec = lax.axis_index("section")
    ex = lax.axis_index("expert")
    y, z = ex // 4, ex % 4

    def turn(v, k):
        return (v + k + 4) % 4

    def dev_y(d):
        return (sec, turn(y, d) * 4 + z)

    def dev_z(d):
        return (sec, y * 4 + turn(z, d))

    sec_next = ((sec + 1) % n_sec, ex)
    sec_prev = ((sec + n_sec - 1) % n_sec, ex)
    DIRS = (1, -1)

    barrier = pltpu.get_barrier_semaphore()
    for dev in (dev_y(1), dev_y(-1), dev_z(1), dev_z(-1), sec_next, sec_prev):
        pl.semaphore_signal(barrier, inc=1, device_id=dev, device_id_type=MESH)

    def span(c):
        return pl.ds(c * width, width)

    def weight_copies(c):
        return (
            pltpu.make_async_copy(w_down.at[:, span(c)], dw.at[c], in_sem.at[0, c]),
            pltpu.make_async_copy(w_gate.at[span(c), :], gw.at[c], in_sem.at[1, c]),
            pltpu.make_async_copy(w_up.at[span(c), :], uw.at[c], in_sem.at[2, c]),
        )

    arrays = (grad, act, saved)

    def source_copy(k, c):
        return pltpu.make_async_copy(
            arrays[k].at[:, span(c)], source.at[:, span(c)], in_sem.at[3 + k, c]
        )

    small = [
        pltpu.make_async_copy(a, b, small_sem.at[i])
        for i, (a, b) in enumerate(
            ((rt_b, routes.at[1]), (rt_f, routes.at[0]), (norm_gain, gain), (router, router_t))
        )
    ]
    small[0].start()
    for c in range(NC):
        source_copy(0, c).start()
    for k in (1, 2, 3):
        small[k].start()

    def msg(src, dst, arrive, ssem, rsem, dev):
        def copy(target):
            return pltpu.make_async_remote_copy(
                src_ref=src, dst_ref=target, send_sem=ssem, recv_sem=rsem,
                device_id=dev, device_id_type=MESH,
            )

        def start():
            copy(dst).start()

        def finish():
            done = copy(arrive)
            done.wait_send()
            done.wait_recv()

        return start, finish

    def start_all(messages):
        for start, _ in messages:
            start()

    def finish_all(messages):
        for _, finish in messages:
            finish()

    COLS = (slice(0, half_w), slice(half_w, width))
    PAIR = (slice(0, 2), slice(2, 4))
    ALL = slice(0, 4)

    def ag_pos(h):
        return ((y, z, dev_y, dev_z), (z, y, dev_z, dev_y))[h]

    def g_at(n, fa, sa, h):
        return gath.at[n, fa, sa, h] if h == 0 else gath.at[n, sa, fa, h]

    def g_cols(n, fa, sa, h, cols):
        if h == 0:
            return gath.at[n, fa, sa, h, :, cols]
        return gath.at[n, sa, fa, h, :, cols]

    def one(stage, n):
        out = []
        for h in range(2):
            f, s, first, _ = ag_pos(h)
            for i, d in enumerate(DIRS):
                sems = (one_s.at[stage, h, i, n], one_r.at[stage, h, i, n], first(d))
                if stage == 0:
                    src = g_at(n, f, s, h)
                    out.append(msg(src, src, g_at(n, turn(f, -d), s, h), *sems))
                else:
                    src = g_cols(n, turn(f, -d), s, h, COLS[i])
                    out.append(msg(src, src, g_cols(n, turn(f, 2), s, h, COLS[i]), *sems))
        return out

    def group(stage, k):
        out = []
        lo, mid, hi = k * NC, k * NC + NC // 2, (k + 1) * NC
        for h in range(2):
            f, s, first, _ = ag_pos(h)
            for i, d in enumerate(DIRS):
                sems = (grp_s.at[k - 1, stage, h, i], grp_r.at[k - 1, stage, h, i], first(d))
                if stage == 0:
                    part_of = slice(lo, hi)
                    src = g_at(part_of, f, s, h)
                    out.append(msg(src, src, g_at(part_of, turn(f, -d), s, h), *sems))
                else:
                    part_of = (slice(lo, mid), slice(mid, hi))[i]
                    src = g_at(part_of, turn(f, -d), s, h)
                    out.append(msg(src, src, g_at(part_of, turn(f, 2), s, h), *sems))
        return out

    def ag3(n):
        out = []
        slot = n % NG
        for h in range(2):
            f, s, _, second = ag_pos(h)
            for i, d in enumerate(DIRS):
                src = g_at(n, ALL, s, h)
                out.append(msg(src, src, g_at(n, ALL, turn(s, -d), h),
                               ag_s.at[0, h, i, slot], ag_r.at[0, h, i, slot], second(d)))
        return out

    def ag4(n):
        out = []
        slot = n % NG
        for h in range(2):
            f, s, _, second = ag_pos(h)
            for i, d in enumerate(DIRS):
                src = g_at(n, PAIR[i], turn(s, -d), h)
                out.append(msg(src, src, g_at(n, PAIR[i], turn(s, 2), h),
                               ag_s.at[1, h, i, slot], ag_r.at[1, h, i, slot], second(d)))
        return out

    def rs_pos(h):
        return ((z, y, dev_z, dev_y), (y, z, dev_y, dev_z))[h]

    def p_idx(slot, fa, sa, h):
        return (slot, sa, fa, h) if h == 0 else (slot, fa, sa, h)

    def rs1(m):
        out = []
        slot = m % NS
        for h in range(2):
            f, s, first, _ = rs_pos(h)
            for i, d in enumerate(DIRS):
                into = r1.at[h, i, slot]
                out.append(msg(part.at[p_idx(slot, turn(f, 2), PAIR[i], h)], into, into,
                               rs_s.at[0, h, i, slot], rs_r.at[0, h, i, slot], first(d)))
        return out

    def rs2(m):
        out = []
        slot = m % NS
        for h in range(2):
            f, s, first, _ = rs_pos(h)
            for i, d in enumerate(DIRS):
                into = r2.at[h, i, slot]
                out.append(msg(part.at[p_idx(slot, turn(f, d), ALL, h)], into, into,
                               rs_s.at[1, h, i, slot], rs_r.at[1, h, i, slot], first(d)))
        return out

    def rs3(m):
        out = []
        slot = m % NS
        for h in range(2):
            f, s, _, second = rs_pos(h)
            for i, d in enumerate(DIRS):
                into = r3.at[h, i, slot]
                out.append(msg(q.at[h, slot, turn(s, 2), :, COLS[i]], into, into,
                               rs_s.at[2, h, i, slot], rs_r.at[2, h, i, slot], second(d)))
        return out

    def rs4(m):
        out = []
        slot = m % NS
        for h in range(2):
            f, s, _, second = rs_pos(h)
            for i, d in enumerate(DIRS):
                into = r4.at[h, i, slot]
                out.append(msg(q.at[h, slot, turn(s, d)], into, into,
                               rs_s.at[3, h, i, slot], rs_r.at[3, h, i, slot], second(d)))
        return out

    def add1(m):
        slot = m % NS
        for h in range(2):
            f = rs_pos(h)[0]
            for i, d in enumerate(DIRS):
                at = p_idx(slot, turn(f, d), PAIR[i], h)
                part[at] = (part[at].astype(F32) + r1[h, i, slot].astype(F32)).astype(BF16)

    def add2(m):
        slot = m % NS
        for h in range(2):
            f = rs_pos(h)[0]
            mine = part[p_idx(slot, f, ALL, h)].astype(F32)
            q[h, slot] = (mine + r2[h, 0, slot].astype(F32) + r2[h, 1, slot].astype(F32)).astype(BF16)

    def add3(m):
        slot = m % NS
        for h in range(2):
            s = rs_pos(h)[1]
            for i, d in enumerate(DIRS):
                to = turn(s, d)
                q[h, slot, to, :, COLS[i]] = (
                    q[h, slot, to, :, COLS[i]].astype(F32) + r3[h, i, slot].astype(F32)
                ).astype(BF16)

    def summed(m, h):
        slot = m % NS
        s = rs_pos(h)[1]
        return (
            q[h, slot, s].astype(F32) + r4[h, 0, slot].astype(F32) + r4[h, 1, slot].astype(F32)
        )

    def sl_msgs(k, stage):
        axis_dev = (dev_z, dev_y)[k]
        if stage == 0:
            return [
                msg(slope.at[k], slope_in.at[k, i], slope_in.at[k, i],
                    sl_s.at[k, i], sl_r.at[k, i], axis_dev(d))
                for i, d in enumerate(DIRS)
            ]
        return [
            msg(slope_in.at[k, 0], slope_in.at[k, 2], slope_in.at[k, 2],
                sl_s.at[k, 2], sl_r.at[k, 2], axis_dev(1))
        ]

    def sl_sum(k):
        slope[k + 1] = slope[k] + slope_in[k, 0] + slope_in[k, 1] + slope_in[k, 2]

    def pass_msgs(which):
        out = []
        for i, (src, dst, dev) in enumerate(
            ((act, act2, sec_next), (grad, grad2, sec_prev), (sel.at[0], sel_f, sec_next), (sel.at[1], sel_b, sec_prev))
        ):
            if i in which:
                out.append(msg(src, dst, dst, pass_s.at[i], pass_r.at[i], dev))
        return out

    row_f_msg = msg(xf, rows_f, rows_f, row_s.at[NC], row_r.at[NC], sec_next)

    def row_b_msg(c):
        return msg(xb.at[c], rows_b.at[c], rows_b.at[c], row_s.at[c], row_r.at[c], sec_prev)

    def lhs(n):
        return gath[n].reshape(rows, width)

    def fwd_rows(i, _):
        at = pl.ds(i * 64, 64)
        g = gacc[at, :]
        activ[at, :] = (g * jax.nn.sigmoid(g) * uacc[at, :]).astype(BF16)
        gacc[at, :] = jnp.zeros((64, hid), F32)
        uacc[at, :] = jnp.zeros((64, hid), F32)
        return 0

    def row_sums(value):
        high = value.astype(BF16)
        low = (value - high.astype(F32)).astype(BF16)
        ones = jnp.ones((8, hid), BF16)
        return lax.dot_general(ones, high, LAST, preferred_element_type=F32) + lax.dot_general(
            ones, low, LAST, preferred_element_type=F32
        )

    def bwd_rows(i, _):
        at = pl.ds(i * 128, 128)
        g = gacc[at, :]
        u = uacc[at, :]
        back = bacc[at, :]
        sig = jax.nn.sigmoid(g)
        silu = g * sig
        prod = (silu * u).astype(BF16).astype(F32) * back
        dgate = (back * u * sig * (1.0 + g * (1.0 - sig))).astype(BF16)
        dup = (back * silu).astype(BF16)
        gcot[at, :] = dgate
        ucot[at, :] = dup
        inner = dgate.astype(F32) * g + dup.astype(F32) * u
        upper = lax.broadcasted_iota(jnp.int32, (8, 128), 0) < 4
        slope[0, :, at] = jnp.where(upper, row_sums(prod), row_sums(inner))
        return 0

    def col(k, h, j):
        return stats[k, h * 16:(h + 1) * 16, j:j + 1]

    def finish_forward(m):
        for h in range(2):
            xf[m, h] = (xf[m, h].astype(F32) + col(0, h, 0) * summed(m, h)).astype(BF16)

    def finish_backward(m):
        c = m - NC
        at = pl.ds(pl.multiple_of(c * width, 128), width)
        router_c = router_t[:, at]
        gain_c = gain[:, at]
        ids = lax.broadcasted_iota(jnp.int32, (16, 8), 1).astype(F32)
        place = lax.broadcasted_iota(jnp.int32, (16, rows), 1)
        row = lax.broadcasted_iota(jnp.int32, (16, rows), 0)
        for h in range(2):
            mine = place == row + (ex * CAP + h * 16)
            slope_col = jnp.sum(jnp.where(mine, slope[2, 0:1, :], 0.0), axis=1, keepdims=True)
            inner_col = jnp.sum(jnp.where(mine, slope[2, 4:5, :], 0.0), axis=1, keepdims=True)
            weight, inv = col(1, h, 0), col(1, h, 1)
            cot = slope_col * col(1, h, 2)
            both = jnp.where(ids == col(1, h, 3), 1.0, 0.0) - jnp.where(ids == col(1, h, 4), 1.0, 0.0)
            dlog = cot * both
            dn = weight * summed(m, h)
            for e in range(8):
                dn = dn + dlog[:, e:e + 1] * router_c[e:e + 1, :]
            coef = inv * inv * (weight * inner_col + cot * col(1, h, 5)) / depth
            change = inv * (dn * gain_c) - coef * xb[c, h].astype(F32)
            xb[c, h] = (gath[c, y, z, h].astype(F32) + change).astype(BF16)
        row_b_msg(c)[0]()

    def halves(value):
        return value.reshape(2, 16, width)

    def pick(onehot, k, c):
        source_copy(k, c).wait()
        return jnp.dot(onehot, source[:, span(c)], preferred_element_type=F32)

    def select(k, onehot, named):
        tok = named.shape[1]
        eye = lax.broadcasted_iota(jnp.int32, (tok, tok), 0) == lax.broadcasted_iota(jnp.int32, (tok, tok), 1)
        sel[k, 0:tok, :] = jnp.where(eye, 1.0 - named, 0.0).astype(BF16)
        sel[k, tok:tok + CAP, :] = onehot

    def onehot_of(k):
        return sel[k, sel.shape[2]:sel.shape[2] + CAP, :]

    def route(k, array, kept):
        onehot = onehot_of(k)
        total = jnp.zeros((CAP, 1), F32)
        for c in range(NC):
            x = pick(onehot, array, c)
            kept[c] = halves(x.astype(BF16))
            total = total + jnp.sum(x * x, axis=1, keepdims=True)
        inverse = lax.rsqrt(total / depth + EPS)
        logits = jnp.zeros((CAP, 8), F32)
        for c in range(NC):
            normed = kept[c].reshape(CAP, width).astype(F32) * inverse * gain[:, span(c)]
            gath[array * NC + c, y, z] = halves(normed.astype(BF16))
            logits = logits + lax.dot_general(
                normed, router_t[:, span(c)], LAST, precision=HI, preferred_element_type=F32
            )
        wide = jnp.concatenate([routes[k].astype(F32), jnp.zeros((6, routes.shape[2]), F32)], axis=0)
        experts = lax.dot_general(onehot, wide.astype(BF16), LAST, preferred_element_type=F32)
        first, second = experts[:, 0:1], experts[:, 1:2]
        ids = lax.broadcasted_iota(jnp.int32, (CAP, 8), 1).astype(F32)
        picked1 = jnp.sum(jnp.where(ids == first, logits, 0.0), axis=1, keepdims=True)
        picked2 = jnp.sum(jnp.where(ids == second, logits, 0.0), axis=1, keepdims=True)
        share = jax.nn.sigmoid(picked1 - picked2)
        on1 = jnp.where(first == 0.0, 1.0, 0.0)
        on2 = jnp.where(second == 0.0, 1.0, 0.0)
        weight = share * on1 + (1.0 - share) * on2
        if k == 1:
            weight = weight.astype(BF16).astype(F32)
        table = jnp.zeros((CAP, 128), F32)
        lane = lax.broadcasted_iota(jnp.int32, (CAP, 128), 1)
        for j, value in enumerate(
            (weight, inverse, (on1 - on2) * share * (1.0 - share), first, second, picked1 - picked2)
        ):
            table = jnp.where(lane == j, value, table)
        stats[k] = table

    small[0].wait()
    onehot_b, named_b = chosen(routes[1])
    pl.semaphore_wait(barrier, 6)
    for c in range(NC):
        gath[c, y, z] = halves(pick(onehot_b, 0, c).astype(BF16))
        start_all(one(0, c))
        source_copy(1, c).start()
    select(1, onehot_b, named_b)
    start_all(pass_msgs((0, 1)))
    for k in (1, 2, 3):
        small[k].wait()
    select(0, *chosen(routes[0]))
    route(0, 1, xf)
    for c in range(NC):
        source_copy(2, c).start()
    for c in range(NC):
        weight_copies(c)[0].start()
    for c in range(NC):
        weight_copies(c)[1].start()
        weight_copies(c)[2].start()
    gacc[...] = jnp.zeros_like(gacc)
    uacc[...] = jnp.zeros_like(uacc)
    bacc[...] = jnp.zeros_like(bacc)

    def when_in(value, low, high):
        return pl.when(jnp.logical_and(value >= low, value < high))

    slope_at = n_ag + 1 + 2 * LAG

    def step(t, _):
        @when_in(t, 0, NC)
        def _():
            finish_all(one(0, t))
            start_all(one(1, t))

        @when_in(t, 1, NC + 1)
        def _():
            finish_all(one(1, t - 1))

        for k, (go, relay, end) in ((1, (1, 3, NC)), (2, (NC, NC + 2, 2 * NC - 1))):
            @pl.when(t == relay)
            def _():
                finish_all(group(0, k))
                start_all(group(1, k))

            @pl.when(t == end)
            def _():
                finish_all(group(1, k))

        @when_in(t, 1, n_ag + 1)
        def _():
            start_all(ag3(t - 1))

        n = t - 1 - LAG

        @when_in(n, 0, n_ag)
        def _():
            finish_all(ag3(n))
            start_all(ag4(n))

        n = t - 1 - 2 * LAG

        @when_in(n, 0, n_ag)
        def _():
            finish_all(ag4(n))

        @pl.when(t == 1)
        def _():
            start_all(group(0, 1))

        @pl.when(t == NC)
        def _():
            start_all(group(0, 2))

        r = t - t_rs

        @when_in(r, 0, n_rs)
        def _():
            start_all(rs1(r))

        m1, m2, m3, m4 = (r - k * LAG for k in (1, 2, 3, 4))

        @when_in(m1, 0, n_rs)
        def _():
            finish_all(rs1(m1))
            add1(m1)
            start_all(rs2(m1))

        @when_in(m2, 0, n_rs)
        def _():
            finish_all(rs2(m2))
            add2(m2)
            start_all(rs3(m2))

        @when_in(m3, 0, n_rs)
        def _():
            finish_all(rs3(m3))
            add3(m3)
            start_all(rs4(m3))

        @when_in(m4, 0, n_rs)
        def _():
            finish_all(rs4(m4))

        @when_in(m4, 0, NC)
        def _():
            finish_forward(m4)

        @pl.when(m4 == NC - 1)
        def _():
            row_f_msg[0]()

        @pl.when(t == slope_at + 0)
        def _():
            start_all(sl_msgs(0, 0))

        @pl.when(t == slope_at + 1)
        def _():
            finish_all(sl_msgs(0, 0))
            start_all(sl_msgs(0, 1))

        @pl.when(t == slope_at + 2)
        def _():
            finish_all(sl_msgs(0, 1))
            sl_sum(0)
            start_all(sl_msgs(1, 0))

        @pl.when(t == slope_at + 3)
        def _():
            finish_all(sl_msgs(1, 0))
            start_all(sl_msgs(1, 1))

        @pl.when(t == slope_at + 4)
        def _():
            finish_all(sl_msgs(1, 1))
            sl_sum(1)

        @when_in(m4, NC, n_rs)
        def _():
            finish_backward(m4)

        @when_in(n, 0, NC)
        def _():
            weight_copies(n)[0].wait()
            bacc[...] += lax.dot_general(lhs(n), dw[n], LAST, preferred_element_type=F32)

        @when_in(n, NC, 2 * NC)
        def _():
            weight_copies(n - NC)[1].wait()
            weight_copies(n - NC)[2].wait()

        @when_in(n, NC, n_ag)
        def _():
            c = n % NC
            gacc[...] += jnp.dot(lhs(n), gw[c], preferred_element_type=F32)
            uacc[...] += jnp.dot(lhs(n), uw[c], preferred_element_type=F32)

        @pl.when(t == NC - 2)
        def _():
            route(1, 2, xb)
            start_all(pass_msgs((2, 3)))

        @pl.when(n == 2 * NC - 1)
        def _():
            lax.fori_loop(0, rows // 64, fwd_rows, 0)

        @pl.when(n == n_ag - 1)
        def _():
            lax.fori_loop(0, rows // 128, bwd_rows, 0)

        m = r + 1
        shape = part.shape[1:]

        @when_in(m, 0, NC)
        def _():
            part[m % NS] = jnp.dot(activ[...], dw[m], preferred_element_type=F32).astype(BF16).reshape(shape)

        @when_in(m, NC, n_rs)
        def _():
            c = m - NC
            value = lax.dot_general(gcot[...], gw[c], LAST, preferred_element_type=F32)
            value = value + lax.dot_general(ucot[...], uw[c], LAST, preferred_element_type=F32)
            part[m % NS] = value.astype(BF16).reshape(shape)

        return 0

    lax.fori_loop(0, t_rs + n_rs + 4 * LAG, step, 0)

    finish_all(pass_msgs((0, 1, 2, 3)))
    row_f_msg[1]()

    def drain(c, _):
        row_b_msg(c)[1]()
        return 0

    lax.fori_loop(0, NC, drain, 0)


def merge_kernel(sel_f, sel_b, act, grad, rows_f, rows_b, out_f, out_b):
    width = rows_f.shape[-1]
    tok = act.shape[0]
    first = (((0,), (0,)), ((), ()))
    for sel, plain, rows, out in ((sel_f, act, rows_f, out_f), (sel_b, grad, rows_b, out_b)):
        for c in range(rows.shape[0]):
            at = slice(c * width, (c + 1) * width)
            moved = lax.dot_general(
                sel[tok:tok + CAP, :], rows[c].reshape(CAP, width), first, preferred_element_type=F32
            )
            stay = lax.dot_general(sel[0:tok, :], plain[:, at], first, preferred_element_type=F32)
            out[:, at] = (moved + stay).astype(BF16)


def local(act_in, saved_in, grad_in, fwd_routes, bwd_routes, w_gate, w_up, w_down, router, norm_gain):
    act, saved, grad = act_in[0], saved_in[0], grad_in[0]
    rt_f, rt_b = fwd_routes[0].T, bwd_routes[0].T
    router_t = router[0].T
    tok, depth = act.shape
    width = depth // NC
    hid = w_gate.shape[2]
    rows = 16 * CAP
    sds = jax.ShapeDtypeStruct
    anywhere = pl.BlockSpec(memory_space=pl.ANY)
    dma = pltpu.SemaphoreType.DMA
    row_shape = (NC, 2, 16, width)
    sel_shape = (tok + CAP, tok)

    V = pltpu.VMEM
    rows_f, rows_b, sel_f, sel_b, act2, grad2 = pl.pallas_call(
        main_kernel,
        out_shape=(
            sds(row_shape, BF16), sds(row_shape, BF16),
            sds(sel_shape, BF16), sds(sel_shape, BF16),
            sds(act.shape, BF16), sds(grad.shape, BF16),
        ),
        in_specs=[anywhere] * 10,
        out_specs=(anywhere,) * 6,
        scratch_shapes=[
            V((tok, depth), BF16), V((2, 2, tok), jnp.int32), V(router_t.shape, F32), V((1, depth), F32),
            V(row_shape, BF16), V(row_shape, BF16), V((2, CAP, 128), F32), V((2,) + sel_shape, BF16),
            V((3 * NC, 4, 4, 2, 16, width), BF16),
            V((NC, width, hid), BF16), V((NC, width, hid), BF16), V((NC, hid, width), BF16),
            V((rows, hid), F32), V((rows, hid), F32), V((rows, hid), F32),
            V((rows, hid), BF16), V((rows, hid), BF16), V((rows, hid), BF16),
            V((NS, 4, 4, 2, 16, width), BF16),
            V((2, 2, NS, 2, 16, width), BF16), V((2, 2, NS, 4, 16, width), BF16),
            V((2, NS, 4, 16, width), BF16),
            V((2, 2, NS, 16, width // 2), BF16), V((2, 2, NS, 16, width), BF16),
            V((3, 8, rows), F32), V((2, 3, 8, rows), F32),
            dma((2, 2, 2, NC)), dma((2, 2, 2, NC)),
            dma((2, 2, 2, 2)), dma((2, 2, 2, 2)),
            dma((2, 2, 2, NG)), dma((2, 2, 2, NG)),
            dma((4, 2, 2, NS)), dma((4, 2, 2, NS)),
            dma((2, 3)), dma((2, 3)),
            dma((6, NC)), dma((4,)), dma((4,)), dma((4,)), dma((NC + 1,)), dma((NC + 1,)),
        ],
        compiler_params=pltpu.CompilerParams(
            collective_id=0, has_side_effects=True, vmem_limit_bytes=67_043_328
        ),
    )(act, saved, grad, rt_f, rt_b, router_t, norm_gain, w_gate[0], w_up[0], w_down[0])

    whole = pl.BlockSpec(sel_shape, lambda c: (0, 0))
    columns = pl.BlockSpec((tok, depth // MERGE), lambda c: (0, c))
    slots = pl.BlockSpec((NC // MERGE, 2, 16, width), lambda c: (c, 0, 0, 0))
    out_f, out_b = pl.pallas_call(
        merge_kernel,
        grid=(MERGE,),
        out_shape=(sds(act.shape, BF16), sds(grad.shape, BF16)),
        in_specs=[whole, whole, columns, columns, slots, slots],
        out_specs=(columns, columns),
    )(sel_f, sel_b, act2, grad2, rows_f, rows_b)
    return (out_f[None], out_b[None])


def solution(mesh):
    in_specs = (
        P("section", "expert", None),
        P("section", "expert", None),
        P("section", "expert", None),
        P("section", "expert", None),
        P("section", "expert", None),
        P("section", None, "expert"),
        P("section", None, "expert"),
        P("section", "expert", None),
        P("section", None, None),
        P("section", None),
    )
    out_specs = (P("section", "expert", None), P("section", "expert", None))
    return jax.shard_map(local, mesh=mesh, in_specs=in_specs, out_specs=out_specs, check_vma=False)
```

```python
import functools

import jax
import jax.numpy as jnp
from jax import lax
from jax.experimental import pallas as pl
from jax.experimental.pallas import tpu as pltpu
from jax.sharding import PartitionSpec as P

EPS = 1e-05
NC = 4
MERGE = 2
CAP = 32
LAG = 2
NS = 2 * LAG + 1
NG = 8
F32 = jnp.float32
BF16 = jnp.bfloat16
MESH = pl.DeviceIdType.MESH
HI = lax.Precision.HIGHEST
LAST = (((1,), (1,)), ((), ()))


def chosen(routes_t):
    tok = routes_t.shape[1]
    named = jnp.max((routes_t == 0).astype(F32), axis=0, keepdims=True)
    before = lax.broadcasted_iota(jnp.int32, (tok, tok), 0) < lax.broadcasted_iota(jnp.int32, (tok, tok), 1)
    wide = jnp.broadcast_to(named, (8, tok)).astype(BF16)
    rank = jnp.dot(wide, before.astype(F32).astype(BF16), preferred_element_type=F32)[0:1]
    slot = lax.broadcasted_iota(jnp.int32, (CAP, tok), 0).astype(F32)
    onehot = jnp.where((slot == rank) & (named > 0.5), 1.0, 0.0).astype(BF16)
    return onehot, named


def main_kernel(
    act, saved, grad, rt_f, rt_b, router, norm_gain, w_gate, w_up, w_down,
    rows_f, rows_b, sel_f, sel_b, act2, grad2,
    source, routes, router_t, gain, xf, xb, stats, sel,
    gath, gw, uw, dw, gacc, uacc, bacc, activ, gcot, ucot,
    part, r1, r2, q, r3, r4, slope, slope_in,
    one_s, one_r, grp_s, grp_r, ag_s, ag_r, rs_s, rs_r, sl_s, sl_r,
    in_sem, small_sem, pass_s, pass_r, row_s, row_r,
):
    width = gath.shape[-1]
    half_w = width // 2
    hid = gacc.shape[1]
    rows = gacc.shape[0]
    depth = gain.shape[1]
    n_ag, n_rs = 3 * NC, 2 * NC
    t_rs = n_ag + 1
    n_sec = lax.axis_size("section")

    sec = lax.axis_index("section")
    ex = lax.axis_index("expert")
    y, z = ex // 4, ex % 4

    def turn(v, k):
        return (v + k + 4) % 4

    def dev_y(d):
        return (sec, turn(y, d) * 4 + z)

    def dev_z(d):
        return (sec, y * 4 + turn(z, d))

    sec_next = ((sec + 1) % n_sec, ex)
    sec_prev = ((sec + n_sec - 1) % n_sec, ex)
    DIRS = (1, -1)

    barrier = pltpu.get_barrier_semaphore()
    for dev in (dev_y(1), dev_y(-1), dev_z(1), dev_z(-1), sec_next, sec_prev):
        pl.semaphore_signal(barrier, inc=1, device_id=dev, device_id_type=MESH)

    def span(c):
        return pl.ds(c * width, width)

    def weight_copies(c):
        return (
            pltpu.make_async_copy(w_down.at[:, span(c)], dw.at[c], in_sem.at[0, c]),
            pltpu.make_async_copy(w_gate.at[span(c), :], gw.at[c], in_sem.at[1, c]),
            pltpu.make_async_copy(w_up.at[span(c), :], uw.at[c], in_sem.at[2, c]),
        )

    arrays = (grad, act, saved)

    def source_copy(k, c):
        return pltpu.make_async_copy(
            arrays[k].at[:, span(c)], source.at[:, span(c)], in_sem.at[3 + k, c]
        )

    small = [
        pltpu.make_async_copy(a, b, small_sem.at[i])
        for i, (a, b) in enumerate(
            ((rt_b, routes.at[1]), (rt_f, routes.at[0]), (norm_gain, gain), (router, router_t))
        )
    ]
    small[0].start()
    for c in range(NC):
        source_copy(0, c).start()
    for k in (1, 2, 3):
        small[k].start()

    def msg(src, dst, arrive, ssem, rsem, dev):
        def copy(target):
            return pltpu.make_async_remote_copy(
                src_ref=src, dst_ref=target, send_sem=ssem, recv_sem=rsem,
                device_id=dev, device_id_type=MESH,
            )

        def start():
            copy(dst).start()

        def finish():
            done = copy(arrive)
            done.wait_send()
            done.wait_recv()

        return start, finish

    def start_all(messages):
        for start, _ in messages:
            start()

    def finish_all(messages):
        for _, finish in messages:
            finish()

    COLS = (slice(0, half_w), slice(half_w, width))
    PAIR = (slice(0, 2), slice(2, 4))
    ALL = slice(0, 4)

    def ag_pos(h):
        return ((y, z, dev_y, dev_z), (z, y, dev_z, dev_y))[h]

    def g_at(n, fa, sa, h):
        return gath.at[n, fa, sa, h] if h == 0 else gath.at[n, sa, fa, h]

    def g_cols(n, fa, sa, h, cols):
        if h == 0:
            return gath.at[n, fa, sa, h, :, cols]
        return gath.at[n, sa, fa, h, :, cols]

    def one(stage, n):
        out = []
        for h in range(2):
            f, s, first, _ = ag_pos(h)
            for i, d in enumerate(DIRS):
                sems = (one_s.at[stage, h, i, n], one_r.at[stage, h, i, n], first(d))
                if stage == 0:
                    src = g_at(n, f, s, h)
                    out.append(msg(src, src, g_at(n, turn(f, -d), s, h), *sems))
                else:
                    src = g_cols(n, turn(f, -d), s, h, COLS[i])
                    out.append(msg(src, src, g_cols(n, turn(f, 2), s, h, COLS[i]), *sems))
        return out

    def group(stage, k):
        out = []
        lo, mid, hi = k * NC, k * NC + NC // 2, (k + 1) * NC
        for h in range(2):
            f, s, first, _ = ag_pos(h)
            for i, d in enumerate(DIRS):
                sems = (grp_s.at[k - 1, stage, h, i], grp_r.at[k - 1, stage, h, i], first(d))
                if stage == 0:
                    part_of = slice(lo, hi)
                    src = g_at(part_of, f, s, h)
                    out.append(msg(src, src, g_at(part_of, turn(f, -d), s, h), *sems))
                else:
                    part_of = (slice(lo, mid), slice(mid, hi))[i]
                    src = g_at(part_of, turn(f, -d), s, h)
                    out.append(msg(src, src, g_at(part_of, turn(f, 2), s, h), *sems))
        return out

    def ag3(n):
        out = []
        slot = n % NG
        for h in range(2):
            f, s, _, second = ag_pos(h)
            for i, d in enumerate(DIRS):
                src = g_at(n, ALL, s, h)
                out.append(msg(src, src, g_at(n, ALL, turn(s, -d), h),
                               ag_s.at[0, h, i, slot], ag_r.at[0, h, i, slot], second(d)))
        return out

    def ag4(n):
        out = []
        slot = n % NG
        for h in range(2):
            f, s, _, second = ag_pos(h)
            for i, d in enumerate(DIRS):
                src = g_at(n, PAIR[i], turn(s, -d), h)
                out.append(msg(src, src, g_at(n, PAIR[i], turn(s, 2), h),
                               ag_s.at[1, h, i, slot], ag_r.at[1, h, i, slot], second(d)))
        return out

    def rs_pos(h):
        return ((z, y, dev_z, dev_y), (y, z, dev_y, dev_z))[h]

    def p_idx(slot, fa, sa, h):
        return (slot, sa, fa, h) if h == 0 else (slot, fa, sa, h)

    def rs1(m, hs=(0, 1)):
        out = []
        slot = m % NS
        for h in hs:
            f, s, first, _ = rs_pos(h)
            for i, d in enumerate(DIRS):
                into = r1.at[h, i, slot]
                out.append(msg(part.at[p_idx(slot, turn(f, 2), PAIR[i], h)], into, into,
                               rs_s.at[0, h, i, slot], rs_r.at[0, h, i, slot], first(d)))
        return out

    def rs2(m, hs=(0, 1)):
        out = []
        slot = m % NS
        for h in hs:
            f, s, first, _ = rs_pos(h)
            for i, d in enumerate(DIRS):
                into = r2.at[h, i, slot]
                out.append(msg(part.at[p_idx(slot, turn(f, d), ALL, h)], into, into,
                               rs_s.at[1, h, i, slot], rs_r.at[1, h, i, slot], first(d)))
        return out

    def rs3(m, hs=(0, 1)):
        out = []
        slot = m % NS
        for h in hs:
            f, s, _, second = rs_pos(h)
            for i, d in enumerate(DIRS):
                into = r3.at[h, i, slot]
                out.append(msg(q.at[h, slot, turn(s, 2), :, COLS[i]], into, into,
                               rs_s.at[2, h, i, slot], rs_r.at[2, h, i, slot], second(d)))
        return out

    def rs4(m, hs=(0, 1)):
        out = []
        slot = m % NS
        for h in hs:
            f, s, _, second = rs_pos(h)
            for i, d in enumerate(DIRS):
                into = r4.at[h, i, slot]
                out.append(msg(q.at[h, slot, turn(s, d)], into, into,
                               rs_s.at[3, h, i, slot], rs_r.at[3, h, i, slot], second(d)))
        return out

    def add1(m, hs):
        slot = m % NS
        for h in hs:
            f = rs_pos(h)[0]
            for i, d in enumerate(DIRS):
                at = p_idx(slot, turn(f, d), PAIR[i], h)
                part[at] = (part[at].astype(F32) + r1[h, i, slot].astype(F32)).astype(BF16)

    def add2(m, hs):
        slot = m % NS
        for h in hs:
            f = rs_pos(h)[0]
            mine = part[p_idx(slot, f, ALL, h)].astype(F32)
            q[h, slot] = (mine + r2[h, 0, slot].astype(F32) + r2[h, 1, slot].astype(F32)).astype(BF16)

    def add3(m, hs):
        slot = m % NS
        for h in hs:
            s = rs_pos(h)[1]
            for i, d in enumerate(DIRS):
                to = turn(s, d)
                q[h, slot, to, :, COLS[i]] = (
                    q[h, slot, to, :, COLS[i]].astype(F32) + r3[h, i, slot].astype(F32)
                ).astype(BF16)

    def summed(m, h):
        slot = m % NS
        s = rs_pos(h)[1]
        return (
            q[h, slot, s].astype(F32) + r4[h, 0, slot].astype(F32) + r4[h, 1, slot].astype(F32)
        )

    def sl_msgs(k, stage):
        axis_dev = (dev_z, dev_y)[k]
        if stage == 0:
            return [
                msg(slope.at[k], slope_in.at[k, i], slope_in.at[k, i],
                    sl_s.at[k, i], sl_r.at[k, i], axis_dev(d))
                for i, d in enumerate(DIRS)
            ]
        return [
            msg(slope_in.at[k, 0], slope_in.at[k, 2], slope_in.at[k, 2],
                sl_s.at[k, 2], sl_r.at[k, 2], axis_dev(1))
        ]

    def sl_sum(k):
        slope[k + 1] = slope[k] + slope_in[k, 0] + slope_in[k, 1] + slope_in[k, 2]

    def pass_msgs(which):
        out = []
        for i, (src, dst, dev) in enumerate(
            ((act, act2, sec_next), (grad, grad2, sec_prev), (sel.at[0], sel_f, sec_next), (sel.at[1], sel_b, sec_prev))
        ):
            if i in which:
                out.append(msg(src, dst, dst, pass_s.at[i], pass_r.at[i], dev))
        return out

    row_f_msg = msg(xf, rows_f, rows_f, row_s.at[NC], row_r.at[NC], sec_next)

    def row_b_msg(c):
        return msg(xb.at[c], rows_b.at[c], rows_b.at[c], row_s.at[c], row_r.at[c], sec_prev)

    def lhs(n):
        return gath[n].reshape(rows, width)

    def fwd_rows(i, _):
        at = pl.ds(i * 64, 64)
        g = gacc[at, :]
        activ[at, :] = (g * jax.nn.sigmoid(g) * uacc[at, :]).astype(BF16)
        gacc[at, :] = jnp.zeros((64, hid), F32)
        uacc[at, :] = jnp.zeros((64, hid), F32)
        return 0

    def row_sums(value):
        high = value.astype(BF16)
        low = (value - high.astype(F32)).astype(BF16)
        ones = jnp.ones((8, hid), BF16)
        return lax.dot_general(ones, high, LAST, preferred_element_type=F32) + lax.dot_general(
            ones, low, LAST, preferred_element_type=F32
        )

    def bwd_rows(i, _):
        at = pl.ds(i * 128, 128)
        g = gacc[at, :]
        u = uacc[at, :]
        back = bacc[at, :]
        sig = jax.nn.sigmoid(g)
        silu = g * sig
        prod = (silu * u).astype(BF16).astype(F32) * back
        dgate = (back * u * sig * (1.0 + g * (1.0 - sig))).astype(BF16)
        dup = (back * silu).astype(BF16)
        gcot[at, :] = dgate
        ucot[at, :] = dup
        inner = dgate.astype(F32) * g + dup.astype(F32) * u
        upper = lax.broadcasted_iota(jnp.int32, (8, 128), 0) < 4
        slope[0, :, at] = jnp.where(upper, row_sums(prod), row_sums(inner))
        return 0

    def col(k, h, j):
        return stats[k, h * 16:(h + 1) * 16, j:j + 1]

    def finish_forward(m):
        for h in range(2):
            xf[m, h] = (xf[m, h].astype(F32) + col(0, h, 0) * summed(m, h)).astype(BF16)

    def finish_backward(m):
        c = m - NC
        at = pl.ds(pl.multiple_of(c * width, 128), width)
        router_c = router_t[:, at]
        gain_c = gain[:, at]
        ids = lax.broadcasted_iota(jnp.int32, (16, 8), 1).astype(F32)
        place = lax.broadcasted_iota(jnp.int32, (16, rows), 1)
        row = lax.broadcasted_iota(jnp.int32, (16, rows), 0)
        for h in range(2):
            mine = place == row + (ex * CAP + h * 16)
            slope_col = jnp.sum(jnp.where(mine, slope[2, 0:1, :], 0.0), axis=1, keepdims=True)
            inner_col = jnp.sum(jnp.where(mine, slope[2, 4:5, :], 0.0), axis=1, keepdims=True)
            weight, inv = col(1, h, 0), col(1, h, 1)
            cot = slope_col * col(1, h, 2)
            both = jnp.where(ids == col(1, h, 3), 1.0, 0.0) - jnp.where(ids == col(1, h, 4), 1.0, 0.0)
            dlog = cot * both
            dn = weight * summed(m, h)
            for e in range(8):
                dn = dn + dlog[:, e:e + 1] * router_c[e:e + 1, :]
            coef = inv * inv * (weight * inner_col + cot * col(1, h, 5)) / depth
            change = inv * (dn * gain_c) - coef * xb[c, h].astype(F32)
            xb[c, h] = (gath[c, y, z, h].astype(F32) + change).astype(BF16)
        row_b_msg(c)[0]()

    def halves(value):
        return value.reshape(2, 16, width)

    def pick(onehot, k, c):
        source_copy(k, c).wait()
        return jnp.dot(onehot, source[:, span(c)], preferred_element_type=F32)

    def select(k, onehot, named):
        tok = named.shape[1]
        eye = lax.broadcasted_iota(jnp.int32, (tok, tok), 0) == lax.broadcasted_iota(jnp.int32, (tok, tok), 1)
        sel[k, 0:tok, :] = jnp.where(eye, 1.0 - named, 0.0).astype(BF16)
        sel[k, tok:tok + CAP, :] = onehot

    def onehot_of(k):
        return sel[k, sel.shape[2]:sel.shape[2] + CAP, :]

    def route(k, array, kept):
        onehot = onehot_of(k)
        total = jnp.zeros((CAP, 1), F32)
        for c in range(NC):
            x = pick(onehot, array, c)
            kept[c] = halves(x.astype(BF16))
            total = total + jnp.sum(x * x, axis=1, keepdims=True)
        inverse = lax.rsqrt(total / depth + EPS)
        logits = jnp.zeros((CAP, 8), F32)
        for c in range(NC):
            normed = kept[c].reshape(CAP, width).astype(F32) * inverse * gain[:, span(c)]
            gath[array * NC + c, y, z] = halves(normed.astype(BF16))
            logits = logits + lax.dot_general(
                normed, router_t[:, span(c)], LAST, precision=HI, preferred_element_type=F32
            )
        wide = jnp.concatenate([routes[k].astype(F32), jnp.zeros((6, routes.shape[2]), F32)], axis=0)
        experts = lax.dot_general(onehot, wide.astype(BF16), LAST, preferred_element_type=F32)
        first, second = experts[:, 0:1], experts[:, 1:2]
        ids = lax.broadcasted_iota(jnp.int32, (CAP, 8), 1).astype(F32)
        picked1 = jnp.sum(jnp.where(ids == first, logits, 0.0), axis=1, keepdims=True)
        picked2 = jnp.sum(jnp.where(ids == second, logits, 0.0), axis=1, keepdims=True)
        share = jax.nn.sigmoid(picked1 - picked2)
        on1 = jnp.where(first == 0.0, 1.0, 0.0)
        on2 = jnp.where(second == 0.0, 1.0, 0.0)
        weight = share * on1 + (1.0 - share) * on2
        if k == 1:
            weight = weight.astype(BF16).astype(F32)
        table = jnp.zeros((CAP, 128), F32)
        lane = lax.broadcasted_iota(jnp.int32, (CAP, 128), 1)
        for j, value in enumerate(
            (weight, inverse, (on1 - on2) * share * (1.0 - share), first, second, picked1 - picked2)
        ):
            table = jnp.where(lane == j, value, table)
        stats[k] = table

    small[0].wait()
    onehot_b, named_b = chosen(routes[1])
    pl.semaphore_wait(barrier, 6)
    for c in range(NC):
        gath[c, y, z] = halves(pick(onehot_b, 0, c).astype(BF16))
        start_all(one(0, c))
        source_copy(1, c).start()
    select(1, onehot_b, named_b)
    start_all(pass_msgs((0, 1)))
    gacc[...] = jnp.zeros_like(gacc)
    uacc[...] = jnp.zeros_like(uacc)
    bacc[...] = jnp.zeros_like(bacc)

    def when_in(value, low, high):
        return pl.when(jnp.logical_and(value >= low, value < high))

    slope_at = n_ag + 1 + 2 * LAG

    def step(t, _):
        @when_in(t, 0, NC)
        def _():
            finish_all(one(0, t))
            start_all(one(1, t))

        @when_in(t, 1, NC + 1)
        def _():
            finish_all(one(1, t - 1))

        for k, (go, relay, end) in ((1, (1, 3, NC)), (2, (NC, NC + 2, 2 * NC - 1))):
            @pl.when(t == relay)
            def _():
                finish_all(group(0, k))
                start_all(group(1, k))

            @pl.when(t == end)
            def _():
                finish_all(group(1, k))

        @when_in(t, 1, n_ag + 1)
        def _():
            start_all(ag3(t - 1))

        n = t - 1 - LAG

        @when_in(n, 0, n_ag)
        def _():
            finish_all(ag3(n))
            start_all(ag4(n))

        n = t - 1 - 2 * LAG

        @when_in(n, 0, n_ag)
        def _():
            finish_all(ag4(n))

        @pl.when(t == 1)
        def _():
            for k in (1, 2, 3):
                small[k].wait()
            select(0, *chosen(routes[0]))
            route(0, 1, xf)
            start_all(group(0, 1))
            for c in range(NC):
                source_copy(2, c).start()
            for c in range(NC):
                weight_copies(c)[0].start()
            for c in range(NC):
                weight_copies(c)[1].start()
                weight_copies(c)[2].start()

        @pl.when(t == NC)
        def _():
            start_all(group(0, 2))

        r = t - t_rs

        @when_in(r, 0, n_rs)
        def _():
            start_all(rs1(r))

        m1, m2, m3, m4 = (r - k * LAG for k in (1, 2, 3, 4))

        @when_in(m1, 0, n_rs)
        def _():
            for h in range(2):
                finish_all(rs1(m1, (h,)))
                add1(m1, (h,))
                start_all(rs2(m1, (h,)))

        @when_in(m2, 0, n_rs)
        def _():
            for h in range(2):
                finish_all(rs2(m2, (h,)))
                add2(m2, (h,))
                start_all(rs3(m2, (h,)))

        @when_in(m3, 0, n_rs)
        def _():
            for h in range(2):
                finish_all(rs3(m3, (h,)))
                add3(m3, (h,))
                start_all(rs4(m3, (h,)))

        @when_in(m4, 0, n_rs)
        def _():
            finish_all(rs4(m4))

        @when_in(m4, 0, NC)
        def _():
            finish_forward(m4)

        @pl.when(m4 == NC - 1)
        def _():
            row_f_msg[0]()

        @pl.when(t == slope_at + 0)
        def _():
            start_all(sl_msgs(0, 0))

        @pl.when(t == slope_at + 1)
        def _():
            finish_all(sl_msgs(0, 0))
            start_all(sl_msgs(0, 1))

        @pl.when(t == slope_at + 2)
        def _():
            finish_all(sl_msgs(0, 1))
            sl_sum(0)
            start_all(sl_msgs(1, 0))

        @pl.when(t == slope_at + 3)
        def _():
            finish_all(sl_msgs(1, 0))
            start_all(sl_msgs(1, 1))

        @pl.when(t == slope_at + 4)
        def _():
            finish_all(sl_msgs(1, 1))
            sl_sum(1)

        @when_in(m4, NC, n_rs)
        def _():
            finish_backward(m4)

        @when_in(n, 0, NC)
        def _():
            weight_copies(n)[0].wait()
            bacc[...] += lax.dot_general(lhs(n), dw[n], LAST, preferred_element_type=F32)

        @when_in(n, NC, 2 * NC)
        def _():
            weight_copies(n - NC)[1].wait()
            weight_copies(n - NC)[2].wait()

        @when_in(n, NC, n_ag)
        def _():
            c = n % NC
            gacc[...] += jnp.dot(lhs(n), gw[c], preferred_element_type=F32)
            uacc[...] += jnp.dot(lhs(n), uw[c], preferred_element_type=F32)

        @pl.when(t == NC - 1)
        def _():
            route(1, 2, xb)
            start_all(pass_msgs((2, 3)))

        @pl.when(n == 2 * NC - 1)
        def _():
            lax.fori_loop(0, rows // 64, fwd_rows, 0)

        @pl.when(n == n_ag - 1)
        def _():
            lax.fori_loop(0, rows // 128, bwd_rows, 0)

        m = r + 1
        shape = part.shape[1:]

        @when_in(m, 0, NC)
        def _():
            part[m % NS] = jnp.dot(activ[...], dw[m], preferred_element_type=F32).astype(BF16).reshape(shape)

        @when_in(m, NC, n_rs)
        def _():
            c = m - NC
            value = lax.dot_general(gcot[...], gw[c], LAST, preferred_element_type=F32)
            value = value + lax.dot_general(ucot[...], uw[c], LAST, preferred_element_type=F32)
            part[m % NS] = value.astype(BF16).reshape(shape)

        return 0

    lax.fori_loop(0, t_rs + n_rs + 4 * LAG, step, 0)

    finish_all(pass_msgs((0, 1, 2, 3)))
    row_f_msg[1]()

    def drain(c, _):
        row_b_msg(c)[1]()
        return 0

    lax.fori_loop(0, NC, drain, 0)


def merge_kernel(sel_f, sel_b, act, grad, rows_f, rows_b, out_f, out_b):
    width = rows_f.shape[-1]
    first = (((0,), (0,)), ((), ()))
    for sel, plain, rows, out in ((sel_f, act, rows_f, out_f), (sel_b, grad, rows_b, out_b)):
        for c in range(rows.shape[0]):
            at = slice(c * width, (c + 1) * width)
            both = jnp.concatenate([plain[:, at], rows[c].reshape(CAP, width)], axis=0)
            out[:, at] = lax.dot_general(sel[...], both, first, preferred_element_type=F32).astype(BF16)


def local(act_in, saved_in, grad_in, fwd_routes, bwd_routes, w_gate, w_up, w_down, router, norm_gain):
    act, saved, grad = act_in[0], saved_in[0], grad_in[0]
    rt_f, rt_b = fwd_routes[0].T, bwd_routes[0].T
    router_t = router[0].T
    tok, depth = act.shape
    width = depth // NC
    hid = w_gate.shape[2]
    rows = 16 * CAP
    sds = jax.ShapeDtypeStruct
    anywhere = pl.BlockSpec(memory_space=pl.ANY)
    dma = pltpu.SemaphoreType.DMA
    row_shape = (NC, 2, 16, width)
    sel_shape = (tok + CAP, tok)

    V = pltpu.VMEM
    rows_f, rows_b, sel_f, sel_b, act2, grad2 = pl.pallas_call(
        main_kernel,
        out_shape=(
            sds(row_shape, BF16), sds(row_shape, BF16),
            sds(sel_shape, BF16), sds(sel_shape, BF16),
            sds(act.shape, BF16), sds(grad.shape, BF16),
        ),
        in_specs=[anywhere] * 10,
        out_specs=(anywhere,) * 6,
        scratch_shapes=[
            V((tok, depth), BF16), V((2, 2, tok), jnp.int32), V(router_t.shape, F32), V((1, depth), F32),
            V(row_shape, BF16), V(row_shape, BF16), V((2, CAP, 128), F32), V((2,) + sel_shape, BF16),
            V((3 * NC, 4, 4, 2, 16, width), BF16),
            V((NC, width, hid), BF16), V((NC, width, hid), BF16), V((NC, hid, width), BF16),
            V((rows, hid), F32), V((rows, hid), F32), V((rows, hid), F32),
            V((rows, hid), BF16), V((rows, hid), BF16), V((rows, hid), BF16),
            V((NS, 4, 4, 2, 16, width), BF16),
            V((2, 2, NS, 2, 16, width), BF16), V((2, 2, NS, 4, 16, width), BF16),
            V((2, NS, 4, 16, width), BF16),
            V((2, 2, NS, 16, width // 2), BF16), V((2, 2, NS, 16, width), BF16),
            V((3, 8, rows), F32), V((2, 3, 8, rows), F32),
            dma((2, 2, 2, NC)), dma((2, 2, 2, NC)),
            dma((2, 2, 2, 2)), dma((2, 2, 2, 2)),
            dma((2, 2, 2, NG)), dma((2, 2, 2, NG)),
            dma((4, 2, 2, NS)), dma((4, 2, 2, NS)),
            dma((2, 3)), dma((2, 3)),
            dma((6, NC)), dma((4,)), dma((4,)), dma((4,)), dma((NC + 1,)), dma((NC + 1,)),
        ],
        compiler_params=pltpu.CompilerParams(
            collective_id=0, has_side_effects=True, vmem_limit_bytes=67_043_328
        ),
    )(act, saved, grad, rt_f, rt_b, router_t, norm_gain, w_gate[0], w_up[0], w_down[0])

    whole = pl.BlockSpec(sel_shape, lambda c: (0, 0))
    columns = pl.BlockSpec((tok, depth // MERGE), lambda c: (0, c))
    slots = pl.BlockSpec((NC // MERGE, 2, 16, width), lambda c: (c, 0, 0, 0))
    out_f, out_b = pl.pallas_call(
        merge_kernel,
        grid=(MERGE,),
        out_shape=(sds(act.shape, BF16), sds(grad.shape, BF16)),
        in_specs=[whole, whole, columns, columns, slots, slots],
        out_specs=(columns, columns),
    )(sel_f, sel_b, act2, grad2, rows_f, rows_b)
    return (out_f[None], out_b[None])


def solution(mesh):
    in_specs = (
        P("section", "expert", None),
        P("section", "expert", None),
        P("section", "expert", None),
        P("section", "expert", None),
        P("section", "expert", None),
        P("section", None, "expert"),
        P("section", None, "expert"),
        P("section", "expert", None),
        P("section", None, None),
        P("section", None),
    )
    out_specs = (P("section", "expert", None), P("section", "expert", None))
    return jax.shard_map(local, mesh=mesh, in_specs=in_specs, out_specs=out_specs, check_vma=False)
```

```python
import functools

import jax
import jax.numpy as jnp
from jax import lax
from jax.experimental import pallas as pl
from jax.experimental.pallas import tpu as pltpu
from jax.sharding import PartitionSpec as P

EPS = 1e-05
NC = 4
MERGE = 2
CAP = 32
LAG = 1
LAG_R = 2
NS = 2 * LAG_R + 1
NG = 8
F32 = jnp.float32
BF16 = jnp.bfloat16
MESH = pl.DeviceIdType.MESH
HI = lax.Precision.HIGHEST
LAST = (((1,), (1,)), ((), ()))


def chosen(routes_t):
    tok = routes_t.shape[1]
    named = jnp.max((routes_t == 0).astype(F32), axis=0, keepdims=True)
    before = lax.broadcasted_iota(jnp.int32, (tok, tok), 0) < lax.broadcasted_iota(jnp.int32, (tok, tok), 1)
    wide = jnp.broadcast_to(named, (8, tok)).astype(BF16)
    rank = jnp.dot(wide, before.astype(F32).astype(BF16), preferred_element_type=F32)[0:1]
    slot = lax.broadcasted_iota(jnp.int32, (CAP, tok), 0).astype(F32)
    onehot = jnp.where((slot == rank) & (named > 0.5), 1.0, 0.0).astype(BF16)
    return onehot, named


def main_kernel(
    act, saved, grad, rt_f, rt_b, router, norm_gain, w_gate, w_up, w_down,
    rows_f, rows_b, sel_f, sel_b, act2, grad2,
    source, routes, router_t, gain, xf, xb, stats, sel,
    gath, gw, uw, dw, gacc, uacc, bacc, activ, gcot, ucot,
    part, r1, r2, q, r3, r4, ready, slope, slope_in,
    one_s, one_r, grp_s, grp_r, ag_s, ag_r, rs_s, rs_r, sl_s, sl_r,
    in_sem, small_sem, pass_s, pass_r, row_s, row_r,
):
    width = gath.shape[-1]
    half_w = width // 2
    hid = gacc.shape[1]
    rows = gacc.shape[0]
    depth = gain.shape[1]
    n_ag, n_rs = 3 * NC, 2 * NC
    t_rs = n_ag - 1
    n_sec = lax.axis_size("section")

    sec = lax.axis_index("section")
    ex = lax.axis_index("expert")
    y, z = ex // 4, ex % 4

    def turn(v, k):
        return (v + k + 4) % 4

    def dev_y(d):
        return (sec, turn(y, d) * 4 + z)

    def dev_z(d):
        return (sec, y * 4 + turn(z, d))

    sec_next = ((sec + 1) % n_sec, ex)
    sec_prev = ((sec + n_sec - 1) % n_sec, ex)
    DIRS = (1, -1)

    barrier = pltpu.get_barrier_semaphore()
    for dev in (dev_y(1), dev_y(-1), dev_z(1), dev_z(-1), sec_next, sec_prev):
        pl.semaphore_signal(barrier, inc=1, device_id=dev, device_id_type=MESH)

    def span(c):
        return pl.ds(c * width, width)

    def weight_copies(c):
        return (
            pltpu.make_async_copy(w_down.at[:, span(c)], dw.at[c], in_sem.at[0, c]),
            pltpu.make_async_copy(w_gate.at[span(c), :], gw.at[c], in_sem.at[1, c]),
            pltpu.make_async_copy(w_up.at[span(c), :], uw.at[c], in_sem.at[2, c]),
        )

    arrays = (grad, act, saved)

    def source_copy(k, c):
        return pltpu.make_async_copy(
            arrays[k].at[:, span(c)], source.at[:, span(c)], in_sem.at[3 + k, c]
        )

    small = [
        pltpu.make_async_copy(a, b, small_sem.at[i])
        for i, (a, b) in enumerate(
            ((rt_b, routes.at[1]), (rt_f, routes.at[0]), (norm_gain, gain), (router, router_t))
        )
    ]
    small[0].start()
    for c in range(NC):
        source_copy(0, c).start()
    for k in (1, 2, 3):
        small[k].start()

    def msg(src, dst, arrive, ssem, rsem, dev):
        def copy(target):
            return pltpu.make_async_remote_copy(
                src_ref=src, dst_ref=target, send_sem=ssem, recv_sem=rsem,
                device_id=dev, device_id_type=MESH,
            )

        def start():
            copy(dst).start()

        def finish():
            done = copy(arrive)
            done.wait_send()
            done.wait_recv()

        return start, finish

    def start_all(messages):
        for start, _ in messages:
            start()

    def finish_all(messages):
        for _, finish in messages:
            finish()

    COLS = (slice(0, half_w), slice(half_w, width))
    PAIR = (slice(0, 2), slice(2, 4))
    ALL = slice(0, 4)

    def ag_pos(h):
        return ((y, z, dev_y, dev_z), (z, y, dev_z, dev_y))[h]

    def g_at(n, fa, sa, h):
        return gath.at[n, fa, sa, h] if h == 0 else gath.at[n, sa, fa, h]

    def g_cols(n, fa, sa, h, cols):
        if h == 0:
            return gath.at[n, fa, sa, h, :, cols]
        return gath.at[n, sa, fa, h, :, cols]

    def one(stage, n):
        out = []
        for h in range(2):
            f, s, first, _ = ag_pos(h)
            for i, d in enumerate(DIRS):
                sems = (one_s.at[stage, h, i, n], one_r.at[stage, h, i, n], first(d))
                if stage == 0:
                    src = g_at(n, f, s, h)
                    out.append(msg(src, src, g_at(n, turn(f, -d), s, h), *sems))
                else:
                    src = g_cols(n, turn(f, -d), s, h, COLS[i])
                    out.append(msg(src, src, g_cols(n, turn(f, 2), s, h, COLS[i]), *sems))
        return out

    def group(stage, k):
        out = []
        lo, mid, hi = k * NC, k * NC + NC // 2, (k + 1) * NC
        for h in range(2):
            f, s, first, _ = ag_pos(h)
            for i, d in enumerate(DIRS):
                sems = (grp_s.at[k - 1, stage, h, i], grp_r.at[k - 1, stage, h, i], first(d))
                if stage == 0:
                    part_of = slice(lo, hi)
                    src = g_at(part_of, f, s, h)
                    out.append(msg(src, src, g_at(part_of, turn(f, -d), s, h), *sems))
                else:
                    part_of = (slice(lo, mid), slice(mid, hi))[i]
                    src = g_at(part_of, turn(f, -d), s, h)
                    out.append(msg(src, src, g_at(part_of, turn(f, 2), s, h), *sems))
        return out

    def ag3(n):
        out = []
        slot = n % NG
        for h in range(2):
            f, s, _, second = ag_pos(h)
            for i, d in enumerate(DIRS):
                src = g_at(n, ALL, s, h)
                out.append(msg(src, src, g_at(n, ALL, turn(s, -d), h),
                               ag_s.at[0, h, i, slot], ag_r.at[0, h, i, slot], second(d)))
        return out

    def ag4(n):
        out = []
        slot = n % NG
        for h in range(2):
            f, s, _, second = ag_pos(h)
            for i, d in enumerate(DIRS):
                src = g_at(n, PAIR[i], turn(s, -d), h)
                out.append(msg(src, src, g_at(n, PAIR[i], turn(s, 2), h),
                               ag_s.at[1, h, i, slot], ag_r.at[1, h, i, slot], second(d)))
        return out

    def rs_pos(h):
        return ((z, y, dev_z, dev_y), (y, z, dev_y, dev_z))[h]

    def p_idx(slot, fa, sa, h):
        return (slot, sa, fa, h) if h == 0 else (slot, fa, sa, h)

    def rs1(m, hs=(0, 1)):
        out = []
        slot = m % NS
        for h in hs:
            f, s, first, _ = rs_pos(h)
            for i, d in enumerate(DIRS):
                into = r1.at[h, i, slot]
                out.append(msg(part.at[p_idx(slot, turn(f, 2), PAIR[i], h)], into, into,
                               rs_s.at[0, h, i, slot], rs_r.at[0, h, i, slot], first(d)))
        return out

    def rs2(m, hs=(0, 1)):
        out = []
        slot = m % NS
        for h in hs:
            f, s, first, _ = rs_pos(h)
            for i, d in enumerate(DIRS):
                into = r2.at[h, i, slot]
                out.append(msg(part.at[p_idx(slot, turn(f, d), ALL, h)], into, into,
                               rs_s.at[1, h, i, slot], rs_r.at[1, h, i, slot], first(d)))
        return out

    def rs3(m, hs=(0, 1)):
        out = []
        slot = m % NS
        for h in hs:
            f, s, _, second = rs_pos(h)
            for i, d in enumerate(DIRS):
                into = r3.at[h, i, slot]
                out.append(msg(q.at[h, slot, turn(s, 2), :, COLS[i]], into, into,
                               rs_s.at[2, h, i, slot], rs_r.at[2, h, i, slot], second(d)))
        return out

    def rs4(m, hs=(0, 1)):
        out = []
        slot = m % NS
        for h in hs:
            f, s, _, second = rs_pos(h)
            for i, d in enumerate(DIRS):
                into = r4.at[h, i, slot]
                out.append(msg(q.at[h, slot, turn(s, d)], into, into,
                               rs_s.at[3, h, i, slot], rs_r.at[3, h, i, slot], second(d)))
        return out

    def add1(m, hs):
        slot = m % NS
        for h in hs:
            f = rs_pos(h)[0]
            for i, d in enumerate(DIRS):
                at = p_idx(slot, turn(f, d), PAIR[i], h)
                part[at] = (part[at].astype(F32) + r1[h, i, slot].astype(F32)).astype(BF16)

    def add2(m, hs):
        slot = m % NS
        for h in hs:
            f = rs_pos(h)[0]
            mine = part[p_idx(slot, f, ALL, h)].astype(F32)
            q[h, slot] = (mine + r2[h, 0, slot].astype(F32) + r2[h, 1, slot].astype(F32)).astype(BF16)

    def add3(m, hs):
        slot = m % NS
        for h in hs:
            s = rs_pos(h)[1]
            for i, d in enumerate(DIRS):
                to = turn(s, d)
                q[h, slot, to, :, COLS[i]] = (
                    q[h, slot, to, :, COLS[i]].astype(F32) + r3[h, i, slot].astype(F32)
                ).astype(BF16)

    def summed(m, h):
        slot = m % NS
        s = rs_pos(h)[1]
        return (
            q[h, slot, s].astype(F32) + r4[h, 0, slot].astype(F32) + r4[h, 1, slot].astype(F32)
        )

    def sl_msgs(k, stage):
        axis_dev = (dev_z, dev_y)[k]
        if stage == 0:
            return [
                msg(slope.at[k], slope_in.at[k, i], slope_in.at[k, i],
                    sl_s.at[k, i], sl_r.at[k, i], axis_dev(d))
                for i, d in enumerate(DIRS)
            ]
        return [
            msg(slope_in.at[k, 0], slope_in.at[k, 2], slope_in.at[k, 2],
                sl_s.at[k, 2], sl_r.at[k, 2], axis_dev(1))
        ]

    def sl_sum(k):
        slope[k + 1] = slope[k] + slope_in[k, 0] + slope_in[k, 1] + slope_in[k, 2]

    def pass_msgs(which):
        out = []
        for i, (src, dst, dev) in enumerate(
            ((act, act2, sec_next), (grad, grad2, sec_prev), (sel.at[0], sel_f, sec_next), (sel.at[1], sel_b, sec_prev))
        ):
            if i in which:
                out.append(msg(src, dst, dst, pass_s.at[i], pass_r.at[i], dev))
        return out

    row_f_msg = msg(xf, rows_f, rows_f, row_s.at[NC], row_r.at[NC], sec_next)

    def row_b_msg(c):
        return msg(xb.at[c], rows_b.at[c], rows_b.at[c], row_s.at[c], row_r.at[c], sec_prev)

    def lhs(n):
        return gath[n].reshape(rows, width)

    def fwd_rows(i, _):
        at = pl.ds(i * 64, 64)
        g = gacc[at, :]
        activ[at, :] = (g * jax.nn.sigmoid(g) * uacc[at, :]).astype(BF16)
        gacc[at, :] = jnp.zeros((64, hid), F32)
        uacc[at, :] = jnp.zeros((64, hid), F32)
        return 0

    def row_sums(value):
        high = value.astype(BF16)
        low = (value - high.astype(F32)).astype(BF16)
        ones = jnp.ones((8, hid), BF16)
        return lax.dot_general(ones, high, LAST, preferred_element_type=F32) + lax.dot_general(
            ones, low, LAST, preferred_element_type=F32
        )

    def bwd_rows(i, _):
        at = pl.ds(i * 128, 128)
        g = gacc[at, :]
        u = uacc[at, :]
        back = bacc[at, :]
        sig = jax.nn.sigmoid(g)
        silu = g * sig
        prod = (silu * u).astype(BF16).astype(F32) * back
        dgate = (back * u * sig * (1.0 + g * (1.0 - sig))).astype(BF16)
        dup = (back * silu).astype(BF16)
        gcot[at, :] = dgate
        ucot[at, :] = dup
        inner = dgate.astype(F32) * g + dup.astype(F32) * u
        upper = lax.broadcasted_iota(jnp.int32, (8, 128), 0) < 4
        slope[0, :, at] = jnp.where(upper, row_sums(prod), row_sums(inner))
        return 0

    def col(k, h, j):
        return stats[k, h * 16:(h + 1) * 16, j:j + 1]

    def finish_forward(m):
        for h in range(2):
            xf[m, h] = (xf[m, h].astype(F32) + col(0, h, 0) * summed(m, h)).astype(BF16)

    def prepare_backward(c):
        at = pl.ds(pl.multiple_of(c * width, 128), width)
        router_c = router_t[:, at]
        gain_c = gain[:, at]
        ids = lax.broadcasted_iota(jnp.int32, (16, 8), 1).astype(F32)
        place = lax.broadcasted_iota(jnp.int32, (16, rows), 1)
        row = lax.broadcasted_iota(jnp.int32, (16, rows), 0)
        for h in range(2):
            mine = place == row + (ex * CAP + h * 16)
            slope_col = jnp.sum(jnp.where(mine, slope[2, 0:1, :], 0.0), axis=1, keepdims=True)
            inner_col = jnp.sum(jnp.where(mine, slope[2, 4:5, :], 0.0), axis=1, keepdims=True)
            weight, inv = col(1, h, 0), col(1, h, 1)
            cot = slope_col * col(1, h, 2)
            both = jnp.where(ids == col(1, h, 3), 1.0, 0.0) - jnp.where(ids == col(1, h, 4), 1.0, 0.0)
            dlog = cot * both
            dn = dlog[:, 0:1] * router_c[0:1, :]
            for e in range(1, 8):
                dn = dn + dlog[:, e:e + 1] * router_c[e:e + 1, :]
            coef = inv * inv * (weight * inner_col + cot * col(1, h, 5)) / depth
            change = inv * (dn * gain_c) - coef * xb[c, h].astype(F32)
            ready[c, h] = gath[c, y, z, h].astype(F32) + change

    def finish_backward(m):
        c = m - NC
        gain_c = gain[:, pl.ds(pl.multiple_of(c * width, 128), width)]
        for h in range(2):
            scale = col(1, h, 0) * col(1, h, 1)
            xb[c, h] = (ready[c, h] + scale * (summed(m, h) * gain_c)).astype(BF16)
        row_b_msg(c)[0]()

    def halves(value):
        return value.reshape(2, 16, width)

    def pick(onehot, k, c):
        source_copy(k, c).wait()
        return jnp.dot(onehot, source[:, span(c)], preferred_element_type=F32)

    def select(k, onehot, named):
        tok = named.shape[1]
        eye = lax.broadcasted_iota(jnp.int32, (tok, tok), 0) == lax.broadcasted_iota(jnp.int32, (tok, tok), 1)
        sel[k, 0:tok, :] = jnp.where(eye, 1.0 - named, 0.0).astype(BF16)
        sel[k, tok:tok + CAP, :] = onehot

    def onehot_of(k):
        return sel[k, sel.shape[2]:sel.shape[2] + CAP, :]

    def route(k, array, kept):
        onehot = onehot_of(k)
        total = jnp.zeros((CAP, 1), F32)
        for c in range(NC):
            x = pick(onehot, array, c)
            kept[c] = halves(x.astype(BF16))
            total = total + jnp.sum(x * x, axis=1, keepdims=True)
        inverse = lax.rsqrt(total / depth + EPS)
        logits = jnp.zeros((CAP, 8), F32)
        for c in range(NC):
            normed = kept[c].reshape(CAP, width).astype(F32) * inverse * gain[:, span(c)]
            gath[array * NC + c, y, z] = halves(normed.astype(BF16))
            logits = logits + lax.dot_general(
                normed, router_t[:, span(c)], LAST, precision=HI, preferred_element_type=F32
            )
        wide = jnp.concatenate([routes[k].astype(F32), jnp.zeros((6, routes.shape[2]), F32)], axis=0)
        experts = lax.dot_general(onehot, wide.astype(BF16), LAST, preferred_element_type=F32)
        first, second = experts[:, 0:1], experts[:, 1:2]
        ids = lax.broadcasted_iota(jnp.int32, (CAP, 8), 1).astype(F32)
        picked1 = jnp.sum(jnp.where(ids == first, logits, 0.0), axis=1, keepdims=True)
        picked2 = jnp.sum(jnp.where(ids == second, logits, 0.0), axis=1, keepdims=True)
        share = jax.nn.sigmoid(picked1 - picked2)
        on1 = jnp.where(first == 0.0, 1.0, 0.0)
        on2 = jnp.where(second == 0.0, 1.0, 0.0)
        weight = share * on1 + (1.0 - share) * on2
        if k == 1:
            weight = weight.astype(BF16).astype(F32)
        table = jnp.zeros((CAP, 128), F32)
        lane = lax.broadcasted_iota(jnp.int32, (CAP, 128), 1)
        for j, value in enumerate(
            (weight, inverse, (on1 - on2) * share * (1.0 - share), first, second, picked1 - picked2)
        ):
            table = jnp.where(lane == j, value, table)
        stats[k] = table

    small[0].wait()
    onehot_b, named_b = chosen(routes[1])
    pl.semaphore_wait(barrier, 6)
    for c in range(NC):
        gath[c, y, z] = halves(pick(onehot_b, 0, c).astype(BF16))
        start_all(one(0, c))
        source_copy(1, c).start()
    select(1, onehot_b, named_b)
    start_all(pass_msgs((0, 1)))
    gacc[...] = jnp.zeros_like(gacc)
    uacc[...] = jnp.zeros_like(uacc)
    bacc[...] = jnp.zeros_like(bacc)

    def when_in(value, low, high):
        return pl.when(jnp.logical_and(value >= low, value < high))

    slope_at = n_ag + 1 + 2 * LAG

    def step(t, _):
        @when_in(t, 0, NC)
        def _():
            finish_all(one(0, t))
            start_all(one(1, t))

        @when_in(t, 1, NC + 1)
        def _():
            finish_all(one(1, t - 1))

        for k, (go, relay, end) in ((1, (1, 3, NC)), (2, (NC, NC + 2, 2 * NC - 1))):
            @pl.when(t == relay)
            def _():
                finish_all(group(0, k))
                start_all(group(1, k))

            @pl.when(t == end)
            def _():
                finish_all(group(1, k))

        @when_in(t, 1, n_ag + 1)
        def _():
            start_all(ag3(t - 1))

        n = t - 1 - LAG

        @when_in(n, 0, n_ag)
        def _():
            finish_all(ag3(n))
            start_all(ag4(n))

        n = t - 1 - 2 * LAG

        @when_in(n, 0, n_ag)
        def _():
            finish_all(ag4(n))

        @pl.when(t == 1)
        def _():
            for k in (1, 2, 3):
                small[k].wait()
            select(0, *chosen(routes[0]))
            route(0, 1, xf)
            start_all(group(0, 1))
            for c in range(NC):
                source_copy(2, c).start()
            for c in range(NC):
                weight_copies(c)[0].start()
            for c in range(NC):
                weight_copies(c)[1].start()
                weight_copies(c)[2].start()

        @pl.when(t == NC)
        def _():
            start_all(group(0, 2))

        r = t - t_rs

        @when_in(r, 0, n_rs)
        def _():
            start_all(rs1(r))

        m1, m2, m3, m4 = (r - k * LAG_R for k in (1, 2, 3, 4))

        @when_in(m1, 0, n_rs)
        def _():
            for h in range(2):
                finish_all(rs1(m1, (h,)))
                add1(m1, (h,))
                start_all(rs2(m1, (h,)))

        @when_in(m2, 0, n_rs)
        def _():
            for h in range(2):
                finish_all(rs2(m2, (h,)))
                add2(m2, (h,))
                start_all(rs3(m2, (h,)))

        @when_in(m3, 0, n_rs)
        def _():
            for h in range(2):
                finish_all(rs3(m3, (h,)))
                add3(m3, (h,))
                start_all(rs4(m3, (h,)))

        @when_in(m4, 0, n_rs)
        def _():
            finish_all(rs4(m4))

        @when_in(m4, 0, NC)
        def _():
            finish_forward(m4)

        @pl.when(m4 == NC - 1)
        def _():
            row_f_msg[0]()

        @pl.when(t == slope_at + 0)
        def _():
            start_all(sl_msgs(0, 0))

        @pl.when(t == slope_at + 1)
        def _():
            finish_all(sl_msgs(0, 0))
            start_all(sl_msgs(0, 1))

        @pl.when(t == slope_at + 2)
        def _():
            finish_all(sl_msgs(0, 1))
            sl_sum(0)
            start_all(sl_msgs(1, 0))

        @pl.when(t == slope_at + 3)
        def _():
            finish_all(sl_msgs(1, 0))
            start_all(sl_msgs(1, 1))

        @pl.when(t == slope_at + 4)
        def _():
            finish_all(sl_msgs(1, 1))
            sl_sum(1)

        @when_in(m4, NC, n_rs)
        def _():
            finish_backward(m4)

        early = t - (slope_at + 5)

        @when_in(early, 0, NC)
        def _():
            prepare_backward(early)

        @when_in(n, 0, NC)
        def _():
            weight_copies(n)[0].wait()
            bacc[...] += lax.dot_general(lhs(n), dw[n], LAST, preferred_element_type=F32)

        @when_in(n, NC, 2 * NC)
        def _():
            weight_copies(n - NC)[1].wait()
            weight_copies(n - NC)[2].wait()

        @when_in(n, NC, n_ag)
        def _():
            c = n % NC
            gacc[...] += jnp.dot(lhs(n), gw[c], preferred_element_type=F32)
            uacc[...] += jnp.dot(lhs(n), uw[c], preferred_element_type=F32)

        @pl.when(t == NC - 1)
        def _():
            route(1, 2, xb)
            start_all(pass_msgs((2, 3)))

        @pl.when(n == 2 * NC - 1)
        def _():
            lax.fori_loop(0, rows // 64, fwd_rows, 0)

        @pl.when(n == n_ag - 1)
        def _():
            lax.fori_loop(0, rows // 128, bwd_rows, 0)

        m = r + 1
        shape = part.shape[1:]

        @when_in(m, 0, NC)
        def _():
            part[m % NS] = jnp.dot(activ[...], dw[m], preferred_element_type=F32).astype(BF16).reshape(shape)

        @when_in(m, NC, n_rs)
        def _():
            c = m - NC
            value = lax.dot_general(gcot[...], gw[c], LAST, preferred_element_type=F32)
            value = value + lax.dot_general(ucot[...], uw[c], LAST, preferred_element_type=F32)
            part[m % NS] = value.astype(BF16).reshape(shape)

        return 0

    lax.fori_loop(0, t_rs + n_rs + 4 * LAG_R, step, 0)

    finish_all(pass_msgs((0, 1, 2, 3)))
    row_f_msg[1]()

    def drain(c, _):
        row_b_msg(c)[1]()
        return 0

    lax.fori_loop(0, NC, drain, 0)


def merge_kernel(sel_f, sel_b, act, grad, rows_f, rows_b, out_f, out_b):
    width = rows_f.shape[-1]
    first = (((0,), (0,)), ((), ()))
    for sel, plain, rows, out in ((sel_f, act, rows_f, out_f), (sel_b, grad, rows_b, out_b)):
        for c in range(rows.shape[0]):
            at = slice(c * width, (c + 1) * width)
            both = jnp.concatenate([plain[:, at], rows[c].reshape(CAP, width)], axis=0)
            out[:, at] = lax.dot_general(sel[...], both, first, preferred_element_type=F32).astype(BF16)


def local(act_in, saved_in, grad_in, fwd_routes, bwd_routes, w_gate, w_up, w_down, router, norm_gain):
    act, saved, grad = act_in[0], saved_in[0], grad_in[0]
    rt_f, rt_b = fwd_routes[0].T, bwd_routes[0].T
    router_t = router[0].T
    tok, depth = act.shape
    width = depth // NC
    hid = w_gate.shape[2]
    rows = 16 * CAP
    sds = jax.ShapeDtypeStruct
    anywhere = pl.BlockSpec(memory_space=pl.ANY)
    dma = pltpu.SemaphoreType.DMA
    row_shape = (NC, 2, 16, width)
    sel_shape = (tok + CAP, tok)

    V = pltpu.VMEM
    rows_f, rows_b, sel_f, sel_b, act2, grad2 = pl.pallas_call(
        main_kernel,
        out_shape=(
            sds(row_shape, BF16), sds(row_shape, BF16),
            sds(sel_shape, BF16), sds(sel_shape, BF16),
            sds(act.shape, BF16), sds(grad.shape, BF16),
        ),
        in_specs=[anywhere] * 10,
        out_specs=(anywhere,) * 6,
        scratch_shapes=[
            V((tok, depth), BF16), V((2, 2, tok), jnp.int32), V(router_t.shape, F32), V((1, depth), F32),
            V(row_shape, BF16), V(row_shape, BF16), V((2, CAP, 128), F32), V((2,) + sel_shape, BF16),
            V((3 * NC, 4, 4, 2, 16, width), BF16),
            V((NC, width, hid), BF16), V((NC, width, hid), BF16), V((NC, hid, width), BF16),
            V((rows, hid), F32), V((rows, hid), F32), V((rows, hid), F32),
            V((rows, hid), BF16), V((rows, hid), BF16), V((rows, hid), BF16),
            V((NS, 4, 4, 2, 16, width), BF16),
            V((2, 2, NS, 2, 16, width), BF16), V((2, 2, NS, 4, 16, width), BF16),
            V((2, NS, 4, 16, width), BF16),
            V((2, 2, NS, 16, width // 2), BF16), V((2, 2, NS, 16, width), BF16),
            V(row_shape, F32), V((3, 8, rows), F32), V((2, 3, 8, rows), F32),
            dma((2, 2, 2, NC)), dma((2, 2, 2, NC)),
            dma((2, 2, 2, 2)), dma((2, 2, 2, 2)),
            dma((2, 2, 2, NG)), dma((2, 2, 2, NG)),
            dma((4, 2, 2, NS)), dma((4, 2, 2, NS)),
            dma((2, 3)), dma((2, 3)),
            dma((6, NC)), dma((4,)), dma((4,)), dma((4,)), dma((NC + 1,)), dma((NC + 1,)),
        ],
        compiler_params=pltpu.CompilerParams(
            collective_id=0, has_side_effects=True, vmem_limit_bytes=67_043_328
        ),
    )(act, saved, grad, rt_f, rt_b, router_t, norm_gain, w_gate[0], w_up[0], w_down[0])

    whole = pl.BlockSpec(sel_shape, lambda c: (0, 0))
    columns = pl.BlockSpec((tok, depth // MERGE), lambda c: (0, c))
    slots = pl.BlockSpec((NC // MERGE, 2, 16, width), lambda c: (c, 0, 0, 0))
    out_f, out_b = pl.pallas_call(
        merge_kernel,
        grid=(MERGE,),
        out_shape=(sds(act.shape, BF16), sds(grad.shape, BF16)),
        in_specs=[whole, whole, columns, columns, slots, slots],
        out_specs=(columns, columns),
    )(sel_f, sel_b, act2, grad2, rows_f, rows_b)
    return (out_f[None], out_b[None])


def solution(mesh):
    in_specs = (
        P("section", "expert", None),
        P("section", "expert", None),
        P("section", "expert", None),
        P("section", "expert", None),
        P("section", "expert", None),
        P("section", None, "expert"),
        P("section", None, "expert"),
        P("section", "expert", None),
        P("section", None, None),
        P("section", None),
    )
    out_specs = (P("section", "expert", None), P("section", "expert", None))
    return jax.shard_map(local, mesh=mesh, in_specs=in_specs, out_specs=out_specs, check_vma=False)
```
